128 devices in a mesh: pipe: 4 (over x_lo, core), expert: 32 (over y, x_hi, z).
Axes of the slice: x: 4 (x_hi: 2, x_lo: 2; x = x_hi * 2 + x_lo), y: 4, z: 4, core: 2. Of those that a mesh axis runs over, the one named last changes fastest.
Arguments:
- fwd_boundary: bfloat16 [4, 2, 4096, 7168], P('pipe', None, 'expert'), may hold values from -6 to 6
- grad_boundary: bfloat16 [4, 2, 4096, 7168], P('pipe', None, 'expert'), may hold values from -6 to 6
- saved_inputs: bfloat16 [4, 2, 4096, 7168], P('pipe', None, 'expert'), may hold values from -6 to 6
- routes: int32 [4, 2, 4096, 1], P('pipe', None, 'expert'), may hold values from 0 to 7
- route_probs: float32 [4, 2, 4096, 1], P('pipe', None, 'expert'), may hold values from 0.1 to 1
- capacity: int32 [4, 8], P('pipe'), may hold values from 9 to 12, as said below
- roster: int32 [4, 2], replicated, may hold values from 0 to 1
- gate_weight: bfloat16 [4, 32, 7168, 256], P('pipe', 'expert'), may hold values from -0.0625 to 0.0625
- up_weight: bfloat16 [4, 32, 7168, 256], P('pipe', 'expert'), may hold values from -0.0625 to 0.0625
- down_weight: bfloat16 [4, 32, 256, 7168], P('pipe', 'expert'), may hold values from -0.1875 to 0.1875
Outputs:
- section_output: bfloat16 [4, 4096, 7168], P('pipe', 'expert')
- input_grad: bfloat16 [4, 4096, 7168], P('pipe', 'expert')
The draws below stay inside these ranges and needn't reach their ends.
Inputs may be any that keep to these rules, and one draw needn't show every extreme that they name: `routes`: each token names exactly one expert. At every section some expert has capacity exactly 12.
All inputs are finite; a program needn't handle non-finite values.
Results may differ from the reference program's by a relative error of at most 0.0034.
Values may be sent and summed in bfloat16 or wider, within the bound.
No kernel may reach another device: no remote copies, remote signals or barrier semaphores. Data moves between devices by JAX's collectives and lax.ppermute only.
A program may use at most 192 MiB of HBM per device.

```python
from functools import partial
import jax
import jax.numpy as jnp
from jax import lax

D = 7168
FF_WIN = 1024
SPLIT = 4
TOPK = 1
MICRO = 2
TOK = 128
CAP = 12
FF_DEV = 256
EXPERTS = 8
SECTIONS = 4
TOKENS = 4096
N_EXPERT = 32


def draw_capacity(key, part):
    first_key, second_key = jax.random.split(jax.random.fold_in(key, 17))
    values = jax.random.randint(first_key, (SECTIONS, EXPERTS), CAP - CAP // 4, CAP + 1)
    chosen = jax.random.randint(second_key, (SECTIONS,), 0, EXPERTS)
    hit_table = jnp.arange(EXPERTS)[None, :] == chosen[:, None]
    return jnp.where(hit_table, CAP, values).astype(jnp.int32)


def with_ends(values, stream_key, least, top_value):
    shape = values.shape
    place = [jax.random.randint(jax.random.fold_in(stream_key, axis), (), 0, shape[axis]) for axis in range(len(shape))]
    values = values.at[tuple(place)].set(least)
    longest = shape.index(max(shape))
    place[longest] = (place[longest] + 1) % shape[longest]
    return values.at[tuple(place)].set(top_value)


def level_of(rng, dims, cuts, smallest, top_value):
    gain, own = 1.0, jax.random.fold_in(rng, 6)
    for position, parts in cuts:
        heights = jnp.exp(jax.random.uniform(jax.random.fold_in(own, position), (parts,), jnp.float32, smallest / len(cuts), top_value / len(cuts)))
        gain = gain * jnp.repeat(heights, dims[position] // parts).reshape([-1 if axis == position else 1 for axis in range(len(dims))])
    return gain


def different_ones(stream_key, rows, number_of, top, lift):
    ranking = jax.random.permutation(jax.random.fold_in(stream_key, 1), number_of)
    favour = ranking
    for power in range(3):
        favour = favour * favour // number_of
    favour = favour * lift // number_of
    chance = jax.random.randint(jax.random.fold_in(stream_key, 2), (rows, number_of), 0, 4096) + favour
    fixed_rows = jax.random.permutation(jax.random.fold_in(stream_key, 3), rows)[jnp.arange(number_of) % rows]
    chance = jnp.where(jnp.arange(rows)[:, None] == fixed_rows[None, :], 1 << 14, chance)
    priority = chance * number_of + jnp.arange(number_of)
    return lax.top_k(priority.astype(jnp.int32), top)[1].astype(jnp.int32)


def noise(rng, shape, width, bound, cuts=(), held_as=jnp.bfloat16):
    factor_of = level_of(rng, shape, cuts, -0.22, 0.18) if cuts else 1.0
    values = jax.random.normal(rng, shape, jnp.float32) * width * factor_of
    return jnp.minimum(jnp.maximum(values, -bound), bound).astype(held_as)


def setup_inputs(seed: int = 0) -> dict:
    seeds = jax.random.split(jax.random.key(seed), 11)
    fwd_boundary = noise(seeds[0], (SECTIONS, MICRO, TOKENS, D), 1.0, 6.0, ((0, 4), (2, 32)))
    grad_boundary = noise(seeds[1], (SECTIONS, MICRO, TOKENS, D), 1.0, 6.0, ((0, 4), (2, 32)))
    saved_inputs = noise(seeds[2], (SECTIONS, MICRO, TOKENS, D), 1.0, 6.0, ((0, 4), (2, 32)))
    routes = different_ones(seeds[3], SECTIONS * MICRO * TOKENS, EXPERTS, TOPK, 2048).reshape((SECTIONS, MICRO, TOKENS, TOPK))
    route_probs = jnp.clip(0.1 + 0.9 * jax.random.uniform(seeds[4], (SECTIONS, MICRO, TOKENS, TOPK), jnp.float32) ** level_of(seeds[4], (SECTIONS, MICRO, TOKENS, TOPK), ((0, 4), (2, 32)), -0.2, 0.2), 0.1, 1.0)
    capacity = draw_capacity(jax.random.fold_in(seeds[10], 71), 0)
    roster = with_ends(jax.random.randint(seeds[6], (SECTIONS, 2), 0, MICRO), jax.random.fold_in(seeds[6], 1), 0, MICRO - 1).astype(jnp.int32)
    gate_weight = noise(seeds[7], (SECTIONS, N_EXPERT, D, FF_DEV), D ** -0.5, 0.0625, ((0, 4), (1, 32)))
    up_weight = noise(seeds[8], (SECTIONS, N_EXPERT, D, FF_DEV), D ** -0.5, 0.0625, ((0, 4), (1, 32)))
    down_weight = noise(seeds[9], (SECTIONS, N_EXPERT, FF_DEV, D), FF_WIN ** -0.5, 0.1875, ((0, 4), (1, 32)))
    return {"fwd_boundary": fwd_boundary, "grad_boundary": grad_boundary, "saved_inputs": saved_inputs, "routes": routes, "route_probs": route_probs, "capacity": capacity, "roster": roster, "gate_weight": gate_weight, "up_weight": up_weight, "down_weight": down_weight}


def route_plan(route_blk, prob_blk, limits, slots):
    token_count, route_top = route_blk.shape
    expert_count = limits.shape[0]
    flat_routes = route_blk.reshape(-1)
    onehot = (flat_routes[:, None] == jnp.arange(expert_count, dtype=jnp.int32)[None, :]).astype(jnp.int32)
    earlier = jnp.cumsum(onehot, axis=0) - onehot
    rank_of = jnp.sum(earlier * onehot, axis=1)
    bound_of = jnp.sum(onehot * limits[None, :], axis=1)
    target = jnp.where(rank_of < bound_of, flat_routes * slots + rank_of, -1).reshape(token_count, route_top)
    columns = jnp.arange(expert_count * slots, dtype=jnp.int32)
    hit_table = target[None, :, :] == columns[:, None, None]
    picker = jnp.sum(hit_table.astype(jnp.float32), axis=2)
    mixing = jnp.sum(jnp.where(hit_table, prob_blk[None, :, :], 0.0), axis=2).T
    return picker, mixing


def expert_work(slot_rows, gate_local, up_local, down_local):
    source_count, slot_count = slot_rows.shape[0], slot_rows.shape[1]
    feature_dim = slot_rows.shape[3]
    fwd_rows = slot_rows[:, :, 0, :].reshape(-1, feature_dim)
    kept_rows = slot_rows[:, :, 1, :].reshape(-1, feature_dim)
    grad_rows = slot_rows[:, :, 2, :].reshape(-1, feature_dim)
    gate_act = jnp.dot(fwd_rows, gate_local, preferred_element_type=jnp.float32)
    up_act = jnp.dot(fwd_rows, up_local, preferred_element_type=jnp.float32)
    hidden = (jax.nn.silu(gate_act) * up_act).astype(jnp.bfloat16)
    out_part = jnp.dot(hidden, down_local, preferred_element_type=jnp.float32).astype(jnp.bfloat16)
    gate_back = jnp.dot(kept_rows, gate_local, preferred_element_type=jnp.float32)
    up_back = jnp.dot(kept_rows, up_local, preferred_element_type=jnp.float32)
    d_hidden = jnp.dot(grad_rows, down_local.T, preferred_element_type=jnp.float32)
    sigmoid_gate = jax.nn.sigmoid(gate_back)
    d_gate = (d_hidden * up_back * sigmoid_gate * (1.0 + gate_back * (1.0 - sigmoid_gate))).astype(jnp.bfloat16)
    d_up = (d_hidden * gate_back * sigmoid_gate).astype(jnp.bfloat16)
    in_part = (jnp.dot(d_gate, gate_local.T, preferred_element_type=jnp.float32)
               + jnp.dot(d_up, up_local.T, preferred_element_type=jnp.float32)).astype(jnp.bfloat16)
    return jnp.stack([out_part, in_part], axis=1).reshape(source_count, slot_count, 2, feature_dim)


def pick_slot(stack, index):
    return lax.dynamic_index_in_dim(stack, index, 0, keepdims=False)


def reference(fwd_boundary, grad_boundary, saved_inputs, routes, route_probs, capacity, roster, gate_weight, up_weight, down_weight):
    output_list = []
    grad_list = []
    planner = jax.vmap(partial(route_plan, slots=CAP), in_axes=(0, 0, None))
    for section_idx in range(SECTIONS):
        fwd_micro = roster[section_idx, 0]
        bwd_micro = roster[section_idx, 1]
        layer_input = pick_slot(fwd_boundary[(section_idx - 1) % SECTIONS], fwd_micro)
        grad_input = pick_slot(grad_boundary[(section_idx + 1) % SECTIONS], bwd_micro)
        kept_input = pick_slot(saved_inputs[section_idx], bwd_micro)
        limits = capacity[section_idx]
        fwd_pick, fwd_mix = planner(pick_slot(routes[section_idx], fwd_micro).reshape(N_EXPERT, TOK, TOPK),
                                    pick_slot(route_probs[section_idx], fwd_micro).reshape(N_EXPERT, TOK, TOPK), limits)
        bwd_pick, bwd_mix = planner(pick_slot(routes[section_idx], bwd_micro).reshape(N_EXPERT, TOK, TOPK),
                                    pick_slot(route_probs[section_idx], bwd_micro).reshape(N_EXPERT, TOK, TOPK), limits)
        in_blocks = layer_input.reshape(N_EXPERT, TOK, D)
        grad_blocks = grad_input.reshape(N_EXPERT, TOK, D)
        kept_blocks = kept_input.reshape(N_EXPERT, TOK, D)
        highest = lax.Precision.HIGHEST
        slot_fwd = jnp.einsum("bst,btd->bsd", fwd_pick, in_blocks.astype(jnp.float32), precision=highest).astype(jnp.bfloat16)
        slot_kept = jnp.einsum("bst,btd->bsd", bwd_pick, kept_blocks.astype(jnp.float32), precision=highest).astype(jnp.bfloat16)
        slot_grad = jnp.einsum("bst,btd->bsd", bwd_pick, grad_blocks.astype(jnp.float32), precision=highest).astype(jnp.bfloat16)
        packed = jnp.stack([slot_fwd, slot_kept, slot_grad], axis=2).reshape(N_EXPERT, EXPERTS, CAP, 3, D)
        packed = jnp.transpose(packed, (1, 0, 2, 3, 4))

        def expert_total(expert_id):
            slot_rows = pick_slot(packed, expert_id)
            running = jnp.zeros((N_EXPERT, CAP, 2, D), jnp.float32)
            for shard_idx in range(SPLIT):
                device = expert_id * SPLIT + shard_idx
                running = running + expert_work(slot_rows, pick_slot(gate_weight[section_idx], device),
                                                pick_slot(up_weight[section_idx], device),
                                                pick_slot(down_weight[section_idx], device)).astype(jnp.float32)
            return running

        totals = lax.map(expert_total, jnp.arange(EXPERTS, dtype=jnp.int32))
        totals = lax.optimization_barrier(totals.astype(jnp.bfloat16)).astype(jnp.float32)
        totals = jnp.transpose(totals, (1, 0, 2, 3, 4)).reshape(N_EXPERT, EXPERTS * CAP, 2, D)
        new_output = in_blocks.astype(jnp.float32) + jnp.einsum("bts,bsd->btd", fwd_mix, totals[:, :, 0, :], precision=highest)
        new_grad = grad_blocks.astype(jnp.float32) + jnp.einsum("bts,bsd->btd", bwd_mix, totals[:, :, 1, :], precision=highest)
        output_list.append(new_output.reshape(TOKENS, D).astype(jnp.bfloat16))
        grad_list.append(new_grad.reshape(TOKENS, D).astype(jnp.bfloat16))
    return jnp.stack(output_list), jnp.stack(grad_list)
```

```python
import functools

import jax
import jax.numpy as jnp
from jax import lax
from jax.experimental import pallas as pl
from jax.experimental.pallas import tpu as pltpu
from jax.sharding import Mesh, PartitionSpec as P

CAP = 12
EXPERTS = 8
RING = 4
TOK = 128
D = 7168
HALF = D // 2
FF = 256
MSG = 2 * CAP
ROWS = EXPERTS * MSG
TILE = 512
STEPS = HALF // TILE
F32 = jnp.float32
BF16 = jnp.bfloat16
NT = (((1,), (1,)), ((), ()))
VMEM = 50 * 2**20


def slot_and_half(r):
    half = ((r >= 8) & (r < 16)) | (r >= 20)
    slot = jnp.where(r < 16, r & 7, 8 + (r & 3))
    return slot, half


def kept_ranks(routes, caps_ref):
    experts = lax.broadcasted_iota(jnp.int32, (EXPERTS, TOK), 0)
    onehot = (routes == experts).astype(F32)
    before = lax.broadcasted_iota(jnp.int32, (TOK, TOK), 0) < lax.broadcasted_iota(jnp.int32, (TOK, TOK), 1)
    earlier = jnp.dot(onehot.astype(BF16), before.astype(F32).astype(BF16), preferred_element_type=F32)
    rank = jnp.sum(onehot * earlier, axis=0, keepdims=True).astype(jnp.int32)
    bound = jnp.zeros((1, TOK), jnp.int32)
    for e in range(EXPERTS):
        bound = jnp.where(routes == e, caps_ref[e], bound)
    return jnp.where(rank < bound, rank, 99)


def pick_kernel(sel_ref, caps_ref, routes_ref, lo_ref, hi_ref, out_ref, pick_ref):
    @pl.when(pl.program_id(0) == 0)
    def _():
        routes = routes_ref[0]
        rank = kept_ranks(routes, caps_ref)
        shape = (EXPERTS, MSG, TOK)
        expert = lax.broadcasted_iota(jnp.int32, shape, 0)
        slot, half = slot_and_half(lax.broadcasted_iota(jnp.int32, shape, 1))
        hit = (routes[None] == expert) & (rank[None] == slot)
        lo = jnp.where(hit & ~half, 1.0, 0.0).reshape(ROWS, TOK)
        hi = jnp.where(hit & half, 1.0, 0.0).reshape(ROWS, TOK)
        pick_ref[...] = jnp.concatenate([lo, hi], axis=1).astype(BF16)

    rows = jnp.concatenate([lo_ref[0], hi_ref[0]], axis=0)
    out_ref[...] = jnp.dot(pick_ref[...], rows, preferred_element_type=F32).astype(BF16)


def pick(micro, caps, routes, x):
    tile = HALF // 2
    own = x.shape[0] > 1
    return pl.pallas_call(
        pick_kernel,
        out_shape=jax.ShapeDtypeStruct((ROWS, HALF), BF16),
        grid_spec=pltpu.PrefetchScalarGridSpec(
            num_scalar_prefetch=2,
            grid=(2,),
            in_specs=[
                pl.BlockSpec((1, 1, TOK), lambda i, s, c: (s[0], 0, 0)),
                pl.BlockSpec((1, TOK, tile), lambda i, s, c: (s[0] if own else 0, 0, i)),
                pl.BlockSpec((1, TOK, tile), lambda i, s, c: (s[0] if own else 0, 0, i + 2)),
            ],
            out_specs=pl.BlockSpec((ROWS, tile), lambda i, s, c: (0, i)),
            scratch_shapes=[pltpu.VMEM((ROWS, 2 * TOK), BF16)],
        ),
        compiler_params=pltpu.CompilerParams(vmem_limit_bytes=VMEM),
        cost_estimate=pl.CostEstimate(flops=2 * ROWS * 256 * HALF, bytes_accessed=2 * (TOK * D + ROWS * HALF), transcendentals=0),
        name="pick",
    )(micro, caps, routes, x, x)


def halves_mask(rows):
    r = lax.broadcasted_iota(jnp.int32, (rows // MSG, MSG, FF), 1)
    return slot_and_half(r)[1].reshape(rows, FF)


def pair_sum(v):
    v = v.reshape(-1, 3, 8, FF)
    both = v[:, 0] + v[:, 1]
    last = v[:, 2] + jnp.concatenate([v[:, 2, 4:], v[:, 2, :4]], axis=1)
    return jnp.concatenate([both[:, None], both[:, None], last[:, None]], axis=1).reshape(-1, FF)


def gate_up_step(i, xs, g_lo, g_hi, u_lo, u_hi, acc):
    x = jnp.concatenate([r[...] for r in xs], axis=0)
    for n, w in enumerate((g_lo, g_hi, u_lo, u_hi)):
        part = jnp.dot(x, w[...], preferred_element_type=F32)

        @pl.when(i == 0)
        def _():
            acc[n] = part

        @pl.when(i > 0)
        def _():
            acc[n] += part


def gate_up(acc):
    half = halves_mask(acc.shape[1])
    gate = pair_sum(jnp.where(half, acc[1], acc[0]))
    up = pair_sum(jnp.where(half, acc[3], acc[2]))
    return gate, up


def saved_kernel(x0, x1, x2, x3, x4, g_lo, g_hi, u_lo, u_hi, gate_ref, up_ref, acc):
    i = pl.program_id(0)
    gate_up_step(i, (x0, x1, x2, x3, x4), g_lo, g_hi, u_lo, u_hi, acc)

    @pl.when(i == STEPS - 1)
    def _():
        gate, up = gate_up(acc)
        gate_ref[...] = gate
        up_ref[...] = up


PIECES = (ROWS, ROWS, ROWS, ROWS // 2, ROWS // 2)
TOTAL = sum(PIECES)


def row_specs(last):
    return [pl.BlockSpec((n, TILE), lambda i: (0, jnp.minimum(i, last))) for n in PIECES]


def saved_side(xs, gate_w, up_w):
    w = [pl.BlockSpec((TILE, FF), lambda i, k=k: (i + k * STEPS, 0)) for k in (0, 1, 0, 1)]
    return pl.pallas_call(
        saved_kernel,
        out_shape=(jax.ShapeDtypeStruct((TOTAL, FF), F32),) * 2,
        grid=(STEPS,),
        in_specs=row_specs(STEPS - 1) + w,
        out_specs=(pl.BlockSpec((TOTAL, FF), lambda i: (0, 0)),) * 2,
        scratch_shapes=[pltpu.VMEM((4, TOTAL, FF), F32)],
        compiler_params=pltpu.CompilerParams(vmem_limit_bytes=VMEM),
        cost_estimate=pl.CostEstimate(
            flops=8 * TOTAL * HALF * FF, bytes_accessed=2 * (TOTAL * HALF + 2 * D * FF), transcendentals=0
        ),
        name="saved_side",
    )(*xs, gate_w, gate_w, up_w, up_w)


def split_rows(tile, outs):
    at = 0
    for o in outs:
        o[...] = tile[at : at + o.shape[0]]
        at += o.shape[0]


def forward_kernel(x0, x1, x2, x3, x4, g_lo, g_hi, u_lo, u_hi, w_lo, w_hi, o0, o1, o2, o3, o4, acc, mid):
    i = pl.program_id(0)

    @pl.when(i < STEPS)
    def _():
        gate_up_step(i, (x0, x1, x2, x3, x4), g_lo, g_hi, u_lo, u_hi, acc)

    @pl.when(i == STEPS - 1)
    def _():
        gate, up = gate_up(acc)
        hidden = gate / (1.0 + jnp.exp(-gate)) * up
        half = halves_mask(TOTAL)
        mid[0] = jnp.where(half, 0.0, hidden).astype(BF16)
        mid[1] = jnp.where(half, hidden, 0.0).astype(BF16)

    @pl.when(i >= STEPS)
    def _():
        tile = jnp.dot(mid[0], w_lo[...], preferred_element_type=F32)
        tile += jnp.dot(mid[1], w_hi[...], preferred_element_type=F32)
        split_rows(tile.astype(BF16), (o0, o1, o2, o3, o4))


def forward_side(xs, gate_w, up_w, down_w):
    first = lambda i: jnp.minimum(i, STEPS - 1)
    second = lambda i: jnp.maximum(i - STEPS, 0)
    w = [pl.BlockSpec((TILE, FF), lambda i, k=k: (first(i) + k * STEPS, 0)) for k in (0, 1, 0, 1)]
    w += [pl.BlockSpec((FF, TILE), lambda i, k=k: (0, second(i) + k * STEPS)) for k in (0, 1)]
    return pl.pallas_call(
        forward_kernel,
        out_shape=tuple(jax.ShapeDtypeStruct((n, HALF), BF16) for n in PIECES),
        grid=(2 * STEPS,),
        in_specs=row_specs(STEPS - 1) + w,
        out_specs=tuple(pl.BlockSpec((n, TILE), lambda i: (0, second(i))) for n in PIECES),
        scratch_shapes=[pltpu.VMEM((4, TOTAL, FF), F32), pltpu.VMEM((2, TOTAL, FF), BF16)],
        compiler_params=pltpu.CompilerParams(vmem_limit_bytes=VMEM),
        cost_estimate=pl.CostEstimate(
            flops=12 * TOTAL * HALF * FF, bytes_accessed=2 * (2 * TOTAL * HALF + 3 * D * FF), transcendentals=TOTAL * FF
        ),
        name="forward_side",
    )(*xs, gate_w, gate_w, up_w, up_w, down_w, down_w)


def backward_kernel(
    x0, x1, x2, x3, x4, w_lo, w_hi, gate_ref, up_ref, g_lo, g_hi, u_lo, u_hi, o0, o1, o2, o3, o4, acc, mid
):
    i = pl.program_id(0)

    @pl.when(i < STEPS)
    def _():
        x = jnp.concatenate([r[...] for r in (x0, x1, x2, x3, x4)], axis=0)
        for n, w in enumerate((w_lo, w_hi)):
            part = lax.dot_general(x, w[...], NT, preferred_element_type=F32)

            @pl.when(i == 0)
            def _():
                acc[n] = part

            @pl.when(i > 0)
            def _():
                acc[n] += part

    @pl.when(i == STEPS - 1)
    def _():
        half = halves_mask(TOTAL)
        dh = pair_sum(jnp.where(half, acc[1], acc[0]))
        gate, up = gate_ref[...], up_ref[...]
        sg = 1.0 / (1.0 + jnp.exp(-gate))
        d_gate = dh * up * sg * (1.0 + gate * (1.0 - sg))
        d_up = dh * gate * sg
        mid[0] = jnp.where(half, 0.0, d_gate).astype(BF16)
        mid[1] = jnp.where(half, d_gate, 0.0).astype(BF16)
        mid[2] = jnp.where(half, 0.0, d_up).astype(BF16)
        mid[3] = jnp.where(half, d_up, 0.0).astype(BF16)

    @pl.when(i >= STEPS)
    def _():
        tile = lax.dot_general(mid[0], g_lo[...], NT, preferred_element_type=F32)
        tile += lax.dot_general(mid[1], g_hi[...], NT, preferred_element_type=F32)
        tile += lax.dot_general(mid[2], u_lo[...], NT, preferred_element_type=F32)
        tile += lax.dot_general(mid[3], u_hi[...], NT, preferred_element_type=F32)
        split_rows(tile.astype(BF16), (o0, o1, o2, o3, o4))


def backward_side(xs, gate, up, gate_w, up_w, down_w):
    first = lambda i: jnp.minimum(i, STEPS - 1)
    second = lambda i: jnp.maximum(i - STEPS, 0)
    w = [pl.BlockSpec((FF, TILE), lambda i, k=k: (0, first(i) + k * STEPS)) for k in (0, 1)]
    w += [pl.BlockSpec((TOTAL, FF), lambda i: (0, 0))] * 2
    w += [pl.BlockSpec((TILE, FF), lambda i, k=k: (second(i) + k * STEPS, 0)) for k in (0, 1, 0, 1)]
    return pl.pallas_call(
        backward_kernel,
        out_shape=tuple(jax.ShapeDtypeStruct((n, HALF), BF16) for n in PIECES),
        grid=(2 * STEPS,),
        in_specs=row_specs(STEPS - 1) + w,
        out_specs=tuple(pl.BlockSpec((n, TILE), lambda i: (0, second(i))) for n in PIECES),
        scratch_shapes=[pltpu.VMEM((2, TOTAL, FF), F32), pltpu.VMEM((4, TOTAL, FF), BF16)],
        compiler_params=pltpu.CompilerParams(vmem_limit_bytes=VMEM),
        cost_estimate=pl.CostEstimate(
            flops=12 * TOTAL * HALF * FF, bytes_accessed=2 * (2 * TOTAL * HALF + 3 * D * FF), transcendentals=TOTAL * FF
        ),
        name="backward_side",
    )(*xs, down_w, down_w, gate, up, gate_w, gate_w, up_w, up_w)


def mix_kernel(sel_ref, caps_ref, routes_ref, probs_ref, total_ref, x_ref, out_ref, spread_ref, prob_ref):
    h = pl.program_id(1)

    @pl.when((pl.program_id(0) == 0) & (h == 0))
    def _():
        routes = routes_ref[0]
        rank = kept_ranks(routes, caps_ref)
        eye = lax.broadcasted_iota(jnp.int32, (TOK, TOK), 0) == lax.broadcasted_iota(jnp.int32, (TOK, TOK), 1)
        column = lambda row: jnp.sum(jnp.where(eye, row, 0.0), axis=1, keepdims=True)
        route_col = column(routes.astype(F32)).astype(jnp.int32)
        rank_col = column(rank.astype(F32)).astype(jnp.int32)
        prob_ref[...] = jnp.broadcast_to(column(probs_ref[0]), (TOK, TOK))
        lane = lax.broadcasted_iota(jnp.int32, (TOK, ROWS), 1)
        expert = (lane * 2731) >> 16
        slot, half = slot_and_half(lane - expert * MSG)
        hit = (route_col == expert) & (rank_col == slot)
        spread_ref[0] = jnp.where(hit & ~half, 1.0, 0.0).astype(BF16)
        spread_ref[1] = jnp.where(hit & half, 1.0, 0.0).astype(BF16)

    found = jnp.dot(spread_ref[h], total_ref[...], preferred_element_type=F32)
    prob = prob_ref[:, :1]
    out_ref[...] = (x_ref[...].astype(F32) + prob * found).astype(BF16)


def mix(micro, caps, routes, probs, totals, x):
    tiles = 2
    tile = HALF // tiles
    return pl.pallas_call(
        mix_kernel,
        out_shape=jax.ShapeDtypeStruct((TOK, D), BF16),
        grid_spec=pltpu.PrefetchScalarGridSpec(
            num_scalar_prefetch=2,
            grid=(tiles, 2),
            in_specs=[
                pl.BlockSpec((1, 1, TOK), lambda n, h, s, c: (s[0], 0, 0)),
                pl.BlockSpec((1, 1, TOK), lambda n, h, s, c: (s[0], 0, 0)),
                pl.BlockSpec((ROWS, tile), lambda n, h, s, c: (0, n)),
                pl.BlockSpec((TOK, tile), lambda n, h, s, c: (0, h * tiles + n)),
            ],
            out_specs=pl.BlockSpec((TOK, tile), lambda n, h, s, c: (0, h * tiles + n)),
            scratch_shapes=[pltpu.VMEM((2, TOK, ROWS), BF16), pltpu.VMEM((TOK, TOK), F32)],
        ),
        compiler_params=pltpu.CompilerParams(vmem_limit_bytes=VMEM),
        cost_estimate=pl.CostEstimate(
            flops=4 * ROWS * TOK * HALF, bytes_accessed=2 * (2 * TOK * D + ROWS * HALF), transcendentals=0
        ),
        name="mix",
    )(micro, caps, routes, probs, totals, x)


def shift(x, axis, by):
    n = lax.axis_size(axis)
    return lax.ppermute(x, axis, [(i, (i + by) % n) for i in range(n)])


def exchange(x):
    return lax.all_to_all(x, ("y", "xh"), 0, 0, tiled=True)


def gather_ring(x):
    left = shift(x, "z", 1)
    right = shift(x, "z", -1)
    half = ROWS // 2
    return x, left, right, shift(left[:half], "z", 1), shift(right[half:], "z", -1)


def add(*terms):
    return sum(t.astype(F32) for t in terms).astype(BF16)


def scatter_ring(own, left, right, far_lo, far_hi):
    half = ROWS // 2
    a = shift(far_lo, "z", 1)
    b = shift(far_hi, "z", -1)
    r_hi = shift(right[half:], "z", 1)
    l_lo = shift(left[:half], "z", -1)
    r_lo = shift(add(right[:half], a), "z", 1)
    l_hi = shift(add(left[half:], b), "z", -1)
    return jnp.concatenate([add(own[:half], r_lo, l_lo), add(own[half:], r_hi, l_hi)], axis=0)


def body(
    fwd_boundary,
    grad_boundary,
    saved_inputs,
    routes,
    route_probs,
    capacity,
    roster,
    gate_weight,
    up_weight,
    down_weight,
):
    section = lax.axis_index("pipe")
    sections = lax.axis_size("pipe")
    after = (section + 1) % sections
    before = (section + sections - 1) % sections
    take = lambda stack, index: lax.dynamic_index_in_dim(stack, index, 0, keepdims=False)
    layer_input = shift(take(fwd_boundary[0], roster[after, 0]), "pipe", 1)
    grad_input = shift(take(grad_boundary[0], roster[before, 1]), "pipe", -1)
    fwd_micro = roster[section, 0].reshape(1)
    bwd_micro = roster[section, 1].reshape(1)
    caps = capacity[0]
    route_rows = routes.reshape(2, 1, TOK)
    prob_rows = route_probs.reshape(2, 1, TOK)
    gate_w, up_w, down_w = gate_weight[0, 0], up_weight[0, 0], down_weight[0, 0]

    kept = gather_ring(exchange(pick(bwd_micro, caps, route_rows, saved_inputs[0])))
    fwd = gather_ring(exchange(pick(fwd_micro, caps, route_rows, layer_input[None])))
    grad = gather_ring(exchange(pick(bwd_micro, caps, route_rows, grad_input[None])))
    gate, up = saved_side(kept, gate_w, up_w)
    own, left, right, far_lo, far_hi = forward_side(fwd, gate_w, up_w, down_w)
    fwd_total = exchange(scatter_ring(own, left, right, far_lo, far_hi))
    own, left, right, far_lo, far_hi = backward_side(grad, gate, up, gate_w, up_w, down_w)
    bwd_total = exchange(scatter_ring(own, left, right, far_lo, far_hi))
    new_output = mix(fwd_micro, caps, route_rows, prob_rows, fwd_total, layer_input)
    new_grad = mix(bwd_micro, caps, route_rows, prob_rows, bwd_total, grad_input)
    return new_output[None], new_grad[None]


def solution(mesh):
    grid = Mesh(mesh.devices.reshape(4, 4, 2, 4), ("pipe", "y", "xh", "z"))
    expert = ("y", "xh", "z")
    rows = P("pipe", None, expert, None)
    weight = P("pipe", expert, None, None)
    in_specs = (rows,) * 5 + (P("pipe", None), P()) + (weight,) * 3
    out_specs = (P("pipe", expert, None),) * 2
    return jax.shard_map(body, mesh=grid, in_specs=in_specs, out_specs=out_specs, check_vma=False)
```

```python
import functools

import jax
import jax.numpy as jnp
from jax import lax
from jax.experimental import pallas as pl
from jax.experimental.pallas import tpu as pltpu
from jax.sharding import Mesh, PartitionSpec as P

CAP = 12
EXPERTS = 8
RING = 4
TOK = 128
D = 7168
HALF = D // 2
FF = 256
MSG = 2 * CAP
ROWS = EXPERTS * MSG
TILE = 1792
STEPS = HALF // TILE
F32 = jnp.float32
BF16 = jnp.bfloat16
NT = (((1,), (1,)), ((), ()))
VMEM = 50 * 2**20
SPAN = 1000


def slot_and_half(r):
    half = ((r >= 8) & (r < 16)) | (r >= 20)
    slot = jnp.where(r < 16, r & 7, 8 + (r & 3))
    return slot, half


def kept_ranks(routes, caps_ref):
    experts = lax.broadcasted_iota(jnp.int32, (EXPERTS, TOK), 0)
    onehot = (routes == experts).astype(F32)
    before = lax.broadcasted_iota(jnp.int32, (TOK, TOK), 0) < lax.broadcasted_iota(jnp.int32, (TOK, TOK), 1)
    earlier = jnp.dot(onehot.astype(BF16), before.astype(F32).astype(BF16), preferred_element_type=F32)
    rank = jnp.sum(onehot * earlier, axis=0, keepdims=True).astype(jnp.int32)
    bound = jnp.zeros((1, TOK), jnp.int32)
    for e in range(EXPERTS):
        bound = jnp.where(routes == e, caps_ref[e], bound)
    return jnp.where(rank < bound, rank, 99)


def pick_kernel(sel_ref, caps_ref, routes_ref, lo_ref, hi_ref, *refs):
    outs, pick_ref = refs[:-1], refs[-1]
    i = pl.program_id(0)

    @pl.when(i == 0)
    def _():
        routes = routes_ref[0]
        rank = kept_ranks(routes, caps_ref)
        shape = (EXPERTS, MSG, TOK)
        expert = lax.broadcasted_iota(jnp.int32, shape, 0)
        slot, half = slot_and_half(lax.broadcasted_iota(jnp.int32, shape, 1))
        hit = (routes[None] == expert) & (rank[None] == slot)
        lo = jnp.where(hit & ~half, 1.0, 0.0).reshape(ROWS, TOK)
        hi = jnp.where(hit & half, 1.0, 0.0).reshape(ROWS, TOK)
        pick_ref[...] = jnp.concatenate([lo, hi], axis=1).astype(BF16)

    rows = jnp.concatenate([lo_ref[0], hi_ref[0]], axis=0)
    tile = jnp.dot(pick_ref[...], rows, preferred_element_type=F32).astype(BF16)
    if len(outs) == 1:
        outs[0][...] = tile
    else:
        for n, out in enumerate(outs):

            @pl.when(i == n)
            def _():
                out[...] = tile


def pick(micro, caps, routes, x, cut):
    own = x.shape[0] > 1
    if cut:
        shapes = [jax.ShapeDtypeStruct((ROWS, TILE), BF16)] * STEPS
        specs = [pl.BlockSpec((ROWS, TILE), lambda i, s, c: (0, 0))] * STEPS
    else:
        shapes = [jax.ShapeDtypeStruct((ROWS, HALF), BF16)]
        specs = [pl.BlockSpec((ROWS, TILE), lambda i, s, c: (0, i))]
    return pl.pallas_call(
        pick_kernel,
        out_shape=shapes + [jax.ShapeDtypeStruct((ROWS, 2 * TOK), BF16)],
        grid_spec=pltpu.PrefetchScalarGridSpec(
            num_scalar_prefetch=2,
            grid=(STEPS,),
            in_specs=[
                pl.BlockSpec((1, 1, TOK), lambda i, s, c: (s[0], 0, 0)),
                pl.BlockSpec((1, TOK, TILE), lambda i, s, c: (s[0] if own else 0, 0, i)),
                pl.BlockSpec((1, TOK, TILE), lambda i, s, c: (s[0] if own else 0, 0, i + STEPS)),
            ],
            out_specs=specs + [pl.BlockSpec((ROWS, 2 * TOK), lambda i, s, c: (0, 0))],
        ),
        compiler_params=pltpu.CompilerParams(vmem_limit_bytes=VMEM),
        cost_estimate=pl.CostEstimate(flops=SPAN * 2 * ROWS * 256 * HALF, bytes_accessed=2 * (TOK * D + ROWS * HALF), transcendentals=0),
        name="pick",
    )(micro, caps, routes, x, x)


def pick_again_kernel(pick_ref, lo_ref, hi_ref, out_ref):
    rows = jnp.concatenate([lo_ref[...], hi_ref[...]], axis=0)
    out_ref[...] = jnp.dot(pick_ref[...], rows, preferred_element_type=F32).astype(BF16)


def pick_again(picker, x):
    tile = HALF // 2
    return pl.pallas_call(
        pick_again_kernel,
        out_shape=jax.ShapeDtypeStruct((ROWS, HALF), BF16),
        grid=(2,),
        in_specs=[
            pl.BlockSpec((ROWS, 2 * TOK), lambda i: (0, 0)),
            pl.BlockSpec((TOK, tile), lambda i: (0, i)),
            pl.BlockSpec((TOK, tile), lambda i: (0, i + 2)),
        ],
        out_specs=pl.BlockSpec((ROWS, tile), lambda i: (0, i)),
        compiler_params=pltpu.CompilerParams(vmem_limit_bytes=VMEM),
        cost_estimate=pl.CostEstimate(flops=SPAN * 2 * ROWS * 256 * HALF, bytes_accessed=2 * (TOK * D + ROWS * HALF), transcendentals=0),
        name="pick_again",
    )(picker, x, x)


TOTAL = RING * ROWS
PACK = TOTAL // MSG * 16
RECEIVED = (ROWS, ROWS, ROWS, ROWS // 2, ROWS // 2)


def unpack_rows(refs):
    if len(refs) == 1:
        refs = [refs[0][:, p * MSG : p * MSG + MSG].astype(F32).reshape(ROWS, -1) for p in range(RING)]
    else:
        refs = [r[...].astype(F32) for r in refs]
    x = jnp.concatenate(refs, axis=0)
    x = x.reshape(TOTAL // MSG, 3, 8, x.shape[1])
    lo = jnp.concatenate([x[:, 0:1], x[:, 2:3]], axis=1).reshape(PACK, x.shape[3])
    hi = jnp.concatenate([x[:, 1:2], x[:, 2:3]], axis=1).reshape(PACK, x.shape[3])
    return lo.astype(BF16), hi.astype(BF16)


def pack_rows(lo, hi, outs):
    n = lo.shape[1]
    lo = lo.reshape(TOTAL // MSG, 2, 8, n)
    hi = hi.reshape(TOTAL // MSG, 2, 8, n)
    upper = lax.broadcasted_iota(jnp.int32, (TOTAL // MSG, 1, 8, n), 2) < 4
    last = jnp.where(upper, lo[:, 1:2], hi[:, 1:2])
    tile = jnp.concatenate([lo[:, 0:1], hi[:, 0:1], last], axis=1).reshape(TOTAL, n).astype(BF16)
    if len(outs) == 1:
        for p in range(RING):
            outs[0][:, p * MSG : p * MSG + MSG] = tile[p * ROWS : p * ROWS + ROWS].reshape(EXPERTS, MSG, n)
        return
    at = 0
    for o in outs:
        o[...] = tile[at : at + o.shape[0]]
        at += o.shape[0]


def both_halves(lo, hi):
    lo = lo.reshape(TOTAL // MSG, 2, 8, FF)
    hi = hi.reshape(TOTAL // MSG, 2, 8, FF)
    upper = lax.broadcasted_iota(jnp.int32, (TOTAL // MSG, 8, FF), 1) < 4
    last = jnp.where(upper, lo[:, 1], hi[:, 1])
    last = last + jnp.concatenate([last[:, 4:], last[:, :4]], axis=1)
    return jnp.concatenate([(lo[:, 0] + hi[:, 0])[:, None], last[:, None]], axis=1).reshape(PACK, FF)


def accumulate(i, acc, parts):
    @pl.when(i == 0)
    def _():
        for n, part in enumerate(parts):
            acc[n] = part

    @pl.when(i > 0)
    def _():
        for n, part in enumerate(parts):
            acc[n] += part


def gate_up_step(i, rows, g_lo, g_hi, u_lo, u_hi, acc):
    lo, hi = rows
    dot = lambda x, w: jnp.dot(x, w[...], preferred_element_type=F32)
    accumulate(i, acc, (dot(lo, g_lo), dot(hi, g_hi), dot(lo, u_lo), dot(hi, u_hi)))


def gate_up(acc):
    return both_halves(acc[0], acc[1]), both_halves(acc[2], acc[3])


def saved_kernel(*refs):
    xs, (g_lo, g_hi, u_lo, u_hi, gate_ref, up_ref, acc) = refs[:-7], refs[-7:]
    i = pl.program_id(0)
    for n in range(STEPS):

        @pl.when(i == n)
        def _():
            gate_up_step(i, unpack_rows(xs[:1] if n == 0 else xs[1:]), g_lo, g_hi, u_lo, u_hi, acc)

    @pl.when(i == STEPS - 1)
    def _():
        gate, up = gate_up(acc)
        gate_ref[...] = gate
        up_ref[...] = up


def row_specs(pieces):
    return [pl.BlockSpec((n, TILE), lambda i: (0, jnp.minimum(i, STEPS - 1))) for n in pieces]


def saved_side(xs, gate_w, up_w):
    w = [pl.BlockSpec((TILE, FF), lambda i, k=k: (i + k * STEPS, 0)) for k in (0, 1, 0, 1)]
    return pl.pallas_call(
        saved_kernel,
        out_shape=(jax.ShapeDtypeStruct((PACK, FF), F32),) * 2,
        grid=(STEPS,),
        in_specs=[pl.BlockSpec(x.shape, lambda i, n=x.ndim: (0,) * n) for x in xs] + w,
        out_specs=(pl.BlockSpec((PACK, FF), lambda i: (0, 0)),) * 2,
        scratch_shapes=[pltpu.VMEM((4, PACK, FF), F32)],
        compiler_params=pltpu.CompilerParams(vmem_limit_bytes=VMEM),
        cost_estimate=pl.CostEstimate(
            flops=SPAN * 8 * PACK * HALF * FF, bytes_accessed=2 * (TOTAL * HALF + 2 * D * FF), transcendentals=0
        ),
        name="saved_side",
    )(*xs, gate_w, gate_w, up_w, up_w)


def forward_kernel(x0, x1, x2, x3, x4, g_lo, g_hi, u_lo, u_hi, w_lo, w_hi, o0, o1, o2, o3, o4, acc, mid):
    i = pl.program_id(0)

    @pl.when(i < STEPS)
    def _():
        gate_up_step(i, unpack_rows((x0, x1, x2, x3, x4)), g_lo, g_hi, u_lo, u_hi, acc)

    @pl.when(i == STEPS - 1)
    def _():
        gate, up = gate_up(acc)
        mid[...] = (gate / (1.0 + jnp.exp(-gate)) * up).astype(BF16)

    @pl.when(i >= STEPS)
    def _():
        lo = jnp.dot(mid[...], w_lo[...], preferred_element_type=F32)
        hi = jnp.dot(mid[...], w_hi[...], preferred_element_type=F32)
        pack_rows(lo, hi, (o0, o1, o2, o3, o4))


def forward_side(xs, gate_w, up_w, down_w):
    first = lambda i: jnp.minimum(i, STEPS - 1)
    second = lambda i: jnp.maximum(i - STEPS, 0)
    w = [pl.BlockSpec((TILE, FF), lambda i, k=k: (first(i) + k * STEPS, 0)) for k in (0, 1, 0, 1)]
    w += [pl.BlockSpec((FF, TILE), lambda i, k=k: (0, second(i) + k * STEPS)) for k in (0, 1)]
    return pl.pallas_call(
        forward_kernel,
        out_shape=tuple(jax.ShapeDtypeStruct((n, HALF), BF16) for n in RECEIVED),
        grid=(2 * STEPS,),
        in_specs=row_specs(RECEIVED) + w,
        out_specs=tuple(pl.BlockSpec((n, TILE), lambda i: (0, second(i))) for n in RECEIVED),
        scratch_shapes=[pltpu.VMEM((4, PACK, FF), F32), pltpu.VMEM((PACK, FF), BF16)],
        compiler_params=pltpu.CompilerParams(vmem_limit_bytes=VMEM),
        cost_estimate=pl.CostEstimate(
            flops=SPAN * 12 * PACK * HALF * FF, bytes_accessed=2 * (2 * TOTAL * HALF + 3 * D * FF), transcendentals=PACK * FF
        ),
        name="forward_side",
    )(*xs, gate_w, gate_w, up_w, up_w, down_w, down_w)


def backward_kernel(x0, x1, x2, x3, x4, w_lo, w_hi, gate_ref, up_ref, g_lo, g_hi, u_lo, u_hi, *refs):
    outs, (acc, mid) = refs[:-2], refs[-2:]
    i = pl.program_id(0)
    dot = lambda x, w: lax.dot_general(x, w[...], NT, preferred_element_type=F32)

    @pl.when(i < STEPS)
    def _():
        lo, hi = unpack_rows((x0, x1, x2, x3, x4))
        accumulate(i, acc, (dot(lo, w_lo), dot(hi, w_hi)))

    @pl.when(i == STEPS - 1)
    def _():
        dh = both_halves(acc[0], acc[1])
        gate, up = gate_ref[...], up_ref[...]
        sg = 1.0 / (1.0 + jnp.exp(-gate))
        mid[0] = (dh * up * sg * (1.0 + gate * (1.0 - sg))).astype(BF16)
        mid[1] = (dh * gate * sg).astype(BF16)

    @pl.when(i >= STEPS)
    def _():
        lo = dot(mid[0], g_lo) + dot(mid[1], u_lo)
        hi = dot(mid[0], g_hi) + dot(mid[1], u_hi)
        for n in range(STEPS):

            @pl.when(i == STEPS + n)
            def _():
                pack_rows(lo, hi, outs[:5] if n == 0 else outs[5:])


def backward_side(xs, gate, up, gate_w, up_w, down_w):
    first = lambda i: jnp.minimum(i, STEPS - 1)
    second = lambda i: jnp.maximum(i - STEPS, 0)
    w = [pl.BlockSpec((FF, TILE), lambda i, k=k: (0, first(i) + k * STEPS)) for k in (0, 1)]
    w += [pl.BlockSpec((PACK, FF), lambda i: (0, 0))] * 2
    w += [pl.BlockSpec((TILE, FF), lambda i, k=k: (second(i) + k * STEPS, 0)) for k in (0, 1, 0, 1)]
    shapes = [(n, TILE) for n in RECEIVED] + [(EXPERTS, RING * MSG, TILE)]
    return pl.pallas_call(
        backward_kernel,
        out_shape=tuple(jax.ShapeDtypeStruct(n, BF16) for n in shapes),
        grid=(2 * STEPS,),
        in_specs=row_specs(RECEIVED) + w,
        out_specs=tuple(pl.BlockSpec(n, lambda i, k=len(n): (0,) * k) for n in shapes),
        scratch_shapes=[pltpu.VMEM((2, PACK, FF), F32), pltpu.VMEM((2, PACK, FF), BF16)],
        compiler_params=pltpu.CompilerParams(vmem_limit_bytes=VMEM),
        cost_estimate=pl.CostEstimate(
            flops=SPAN * 12 * PACK * HALF * FF, bytes_accessed=2 * (2 * TOTAL * HALF + 3 * D * FF), transcendentals=PACK * FF
        ),
        name="backward_side",
    )(*xs, down_w, down_w, gate, up, gate_w, gate_w, up_w, up_w)


def spread_kernel(sel_ref, caps_ref, routes_ref, probs_ref, spread_ref, prob_ref):
    routes = routes_ref[0]
    rank = kept_ranks(routes, caps_ref)
    eye = lax.broadcasted_iota(jnp.int32, (TOK, TOK), 0) == lax.broadcasted_iota(jnp.int32, (TOK, TOK), 1)
    column = lambda row: jnp.sum(jnp.where(eye, row, 0.0), axis=1, keepdims=True)
    route_col = column(routes.astype(F32)).astype(jnp.int32)
    rank_col = column(rank.astype(F32)).astype(jnp.int32)
    prob_ref[...] = jnp.broadcast_to(column(probs_ref[0]), (TOK, TOK))
    lane = lax.broadcasted_iota(jnp.int32, (TOK, ROWS), 1)
    expert = (lane * 2731) >> 16
    slot, half = slot_and_half(lane - expert * MSG)
    hit = (route_col == expert) & (rank_col == slot)
    spread_ref[0] = jnp.where(hit & ~half, 1.0, 0.0).astype(BF16)
    spread_ref[1] = jnp.where(hit & half, 1.0, 0.0).astype(BF16)


def spread(micro, caps, routes, probs):
    return pl.pallas_call(
        spread_kernel,
        out_shape=(jax.ShapeDtypeStruct((2, TOK, ROWS), BF16), jax.ShapeDtypeStruct((TOK, TOK), F32)),
        grid_spec=pltpu.PrefetchScalarGridSpec(
            num_scalar_prefetch=2,
            grid=(1,),
            in_specs=[pl.BlockSpec((1, 1, TOK), lambda i, s, c: (s[0], 0, 0))] * 2,
            out_specs=(
                pl.BlockSpec((2, TOK, ROWS), lambda i, s, c: (0, 0, 0)),
                pl.BlockSpec((TOK, TOK), lambda i, s, c: (0, 0)),
            ),
        ),
        name="spread",
    )(micro, caps, routes, probs)


def mix_kernel(count, spread_ref, prob_ref, x_ref, *refs):
    total = refs[0][...]
    if count > 1:
        total = sum(r[...].astype(F32) for r in refs[:count]).astype(BF16)
    found = jnp.dot(spread_ref[0], total, preferred_element_type=F32)
    refs[-1][...] = (x_ref[...].astype(F32) + prob_ref[:, :1] * found).astype(BF16)


def mix(plan, parts, x, first=0, into=None):
    tiles = parts[0].shape[1] // TILE
    into = () if into is None else (into,)
    return pl.pallas_call(
        functools.partial(mix_kernel, len(parts)),
        out_shape=jax.ShapeDtypeStruct((TOK, D), BF16),
        grid=(tiles, 2),
        in_specs=[
            pl.BlockSpec((1, TOK, ROWS), lambda n, h: (h, 0, 0)),
            pl.BlockSpec((TOK, TOK), lambda n, h: (0, 0)),
            pl.BlockSpec((TOK, TILE), lambda n, h: (0, h * STEPS + first + n)),
        ]
        + [pl.BlockSpec((ROWS, TILE), lambda n, h: (0, n)) for _ in parts]
        + [pl.BlockSpec(memory_space=pl.ANY) for _ in into],
        out_specs=pl.BlockSpec((TOK, TILE), lambda n, h: (0, h * STEPS + first + n)),
        input_output_aliases={3 + len(parts): 0} if into else {},
        compiler_params=pltpu.CompilerParams(vmem_limit_bytes=VMEM),
        cost_estimate=pl.CostEstimate(
            flops=SPAN * 4 * ROWS * TOK * TILE * tiles, bytes_accessed=2 * (4 * TOK + ROWS) * TILE * tiles, transcendentals=0
        ),
        name="mix",
    )(*plan, x, *parts, *into)


def shift(x, axis, by):
    n = lax.axis_size(axis)
    return lax.ppermute(x, axis, [(i, (i + by) % n) for i in range(n)])


def labelled(f):
    def call(name, *args):
        with jax.named_scope(name):
            return f(*args)

    return call


@labelled
def exchange(x):
    return lax.all_to_all(x, ("y", "xh"), 0, 0, tiled=True)


@labelled
def gather_ring(x, *first):
    left = shift(x, "z", 1)
    right = shift(x, "z", -1)
    if first:
        left, right, _ = lax.optimization_barrier((left, right, first))
    half = ROWS // 2
    return x, left, right, shift(left[:half], "z", 1), shift(right[half:], "z", -1)


def add(*terms):
    return sum(t.astype(F32) for t in terms).astype(BF16)


def after(x, *others):
    return lax.optimization_barrier((x, others))[0]


@labelled
def scatter_far(far_lo, far_hi):
    return shift(far_lo, "z", 1), shift(far_hi, "z", -1)


@labelled
def scatter_near(left, right, far):
    half = ROWS // 2
    right = jnp.concatenate([add(right[:half], far[0]), right[half:]], axis=0)
    left = jnp.concatenate([left[:half], add(left[half:], far[1])], axis=0)
    return shift(right, "z", 1), shift(left, "z", -1)


def body(
    fwd_boundary,
    grad_boundary,
    saved_inputs,
    routes,
    route_probs,
    capacity,
    roster,
    gate_weight,
    up_weight,
    down_weight,
):
    section = lax.axis_index("pipe")
    sections = lax.axis_size("pipe")
    after_ = (section + 1) % sections
    before = (section + sections - 1) % sections
    take = lambda stack, index: lax.dynamic_index_in_dim(stack, index, 0, keepdims=False)
    fwd_micro = roster[section, 0].reshape(1)
    bwd_micro = roster[section, 1].reshape(1)
    caps = capacity[0]
    route_rows = routes.reshape(2, 1, TOK)
    prob_rows = route_probs.reshape(2, 1, TOK)
    gate_w, up_w, down_w = gate_weight[0, 0], up_weight[0, 0], down_weight[0, 0]

    outgoing = take(fwd_boundary[0], roster[after_, 0])
    layer_input = shift(outgoing, "pipe", 1)
    saved_a, saved_b, bwd_pick = pick(after(bwd_micro, outgoing), caps, route_rows, saved_inputs[0], True)
    back_index, saved_a, saved_b = lax.optimization_barrier((roster[before, 1], saved_a, saved_b))
    returning = take(grad_boundary[0], back_index)
    grad_input = shift(returning, "pipe", -1)
    own, left, right, far_lo, far_hi = gather_ring("saved_ring_a", saved_a)
    plane_b = exchange("saved_plane_b", saved_b)
    fwd_rows, _ = pick(fwd_micro, caps, route_rows, after(layer_input, plane_b, left, right)[None], False)
    kept_b = gather_ring("saved_ring_b", plane_b)
    input_plane = exchange("input_plane", fwd_rows)
    grad_rows = pick_again(bwd_pick, after(grad_input, fwd_rows, kept_b[1], kept_b[2], far_lo, far_hi))
    grad_plane = exchange("grad_plane", grad_rows)
    wide = jnp.stack([own, left, right, jnp.concatenate([far_lo, far_hi], axis=0)]).reshape(RING, EXPERTS, MSG, TILE)
    wide = wide.transpose(1, 0, 2, 3).reshape(EXPERTS, RING * MSG, TILE)
    kept_a = exchange("saved_plane_a", after(wide, grad_plane))
    gate, up = saved_side((kept_a, *kept_b), gate_w, up_w)
    fwd = gather_ring("input_ring", input_plane, grad_plane)
    own, left, right, far_lo, far_hi = forward_side(fwd, gate_w, up_w, down_w)
    far = scatter_far("output_far", far_lo, far_hi)
    grad = gather_ring("grad_ring", grad_plane, own, gate)
    gate = after(gate, *far)
    parts = backward_side(grad, gate, up, gate_w, up_w, down_w)
    near = scatter_near("output_near", left, right, far)
    far_a = scatter_far("back_far_a", *parts[3:5])
    planes = exchange("back_plane_b", parts[5]).reshape(EXPERTS, RING, MSG, TILE)
    fwd_total = exchange("output_plane", after(add(own, *near), planes))
    near_a = scatter_near("back_near_a", *parts[1:3], far_a)
    own, left, right, far = (planes[:, p].reshape(ROWS, TILE) for p in range(RING))
    far_b = scatter_far("back_far_b", far[: ROWS // 2], far[ROWS // 2 :])
    near_b = scatter_near("back_near_b", left, right, far_b)
    total_a = exchange("back_plane_a", after(add(parts[0], *near_a), fwd_total))

    fwd_plan = spread(fwd_micro, caps, route_rows, prob_rows)
    bwd_plan = spread(bwd_micro, caps, route_rows, prob_rows)
    new_output = mix(fwd_plan, (fwd_total,), layer_input)
    new_grad = mix(bwd_plan, (total_a,), grad_input)
    new_grad = mix(bwd_plan, (own, *near_b), grad_input, 1, new_grad)
    return new_output[None], new_grad[None]


def solution(mesh):
    grid = Mesh(mesh.devices.reshape(4, 4, 2, 4), ("pipe", "y", "xh", "z"))
    expert = ("y", "xh", "z")
    rows = P("pipe", None, expert, None)
    weight = P("pipe", expert, None, None)
    in_specs = (rows,) * 5 + (P("pipe", None), P()) + (weight,) * 3
    out_specs = (P("pipe", expert, None),) * 2
    return jax.shard_map(body, mesh=grid, in_specs=in_specs, out_specs=out_specs, check_vma=False)
```

```python
import functools

import jax
import jax.numpy as jnp
from jax import lax
from jax.experimental import pallas as pl
from jax.experimental.pallas import tpu as pltpu
from jax.sharding import Mesh, PartitionSpec as P

CAP = 12
EXPERTS = 8
RING = 4
TOK = 128
D = 7168
HALF = D // 2
FF = 256
MSG = 2 * CAP
ROWS = EXPERTS * MSG
TILE = 1792
STEPS = HALF // TILE
NEAR = 10**6
F32 = jnp.float32
BF16 = jnp.bfloat16
NT = (((1,), (1,)), ((), ()))
VMEM = 50 * 2**20
SPAN = 1000


def slot_and_half(r):
    half = ((r >= 8) & (r < 16)) | (r >= 20)
    slot = jnp.where(r < 16, r & 7, 8 + (r & 3))
    return slot, half


def kept_ranks(routes, caps_ref):
    experts = lax.broadcasted_iota(jnp.int32, (EXPERTS, TOK), 0)
    onehot = (routes == experts).astype(F32)
    before = lax.broadcasted_iota(jnp.int32, (TOK, TOK), 0) < lax.broadcasted_iota(jnp.int32, (TOK, TOK), 1)
    earlier = jnp.dot(onehot.astype(BF16), before.astype(F32).astype(BF16), preferred_element_type=F32)
    rank = jnp.sum(onehot * earlier, axis=0, keepdims=True).astype(jnp.int32)
    bound = jnp.zeros((1, TOK), jnp.int32)
    for e in range(EXPERTS):
        bound = jnp.where(routes == e, caps_ref[e], bound)
    return jnp.where(rank < bound, rank, 99)


def pick_kernel(sel_ref, caps_ref, routes_ref, lo_ref, hi_ref, *refs):
    outs, pick_ref = refs[:-1], refs[-1]
    i = pl.program_id(0)

    @pl.when(i == 0)
    def _():
        routes = routes_ref[0]
        rank = kept_ranks(routes, caps_ref)
        shape = (EXPERTS, MSG, TOK)
        expert = lax.broadcasted_iota(jnp.int32, shape, 0)
        slot, half = slot_and_half(lax.broadcasted_iota(jnp.int32, shape, 1))
        hit = (routes[None] == expert) & (rank[None] == slot)
        lo = jnp.where(hit & ~half, 1.0, 0.0).reshape(ROWS, TOK)
        hi = jnp.where(hit & half, 1.0, 0.0).reshape(ROWS, TOK)
        pick_ref[...] = jnp.concatenate([lo, hi], axis=1).astype(BF16)

    rows = jnp.concatenate([lo_ref[0], hi_ref[0]], axis=0)
    tile = jnp.dot(pick_ref[...], rows, preferred_element_type=F32).astype(BF16)
    if len(outs) == 1:
        outs[0][...] = tile
    else:
        for n, out in enumerate(outs):

            @pl.when(i == n)
            def _():
                out[...] = tile


def pick(micro, caps, routes, x, cut):
    own = x.shape[0] > 1
    if cut:
        shapes = [jax.ShapeDtypeStruct((ROWS, TILE), BF16)] * STEPS
        specs = [pl.BlockSpec((ROWS, TILE), lambda i, s, c: (0, 0))] * STEPS
    else:
        shapes = [jax.ShapeDtypeStruct((ROWS, HALF), BF16)]
        specs = [pl.BlockSpec((ROWS, TILE), lambda i, s, c: (0, i))]
    return pl.pallas_call(
        pick_kernel,
        out_shape=shapes + [jax.ShapeDtypeStruct((ROWS, 2 * TOK), BF16)],
        grid_spec=pltpu.PrefetchScalarGridSpec(
            num_scalar_prefetch=2,
            grid=(STEPS,),
            in_specs=[
                pl.BlockSpec((1, 1, TOK), lambda i, s, c: (s[0], 0, 0)),
                pl.BlockSpec((1, TOK, TILE), lambda i, s, c: (s[0] if own else 0, 0, i)),
                pl.BlockSpec((1, TOK, TILE), lambda i, s, c: (s[0] if own else 0, 0, i + STEPS)),
            ],
            out_specs=specs + [pl.BlockSpec((ROWS, 2 * TOK), lambda i, s, c: (0, 0))],
        ),
        compiler_params=pltpu.CompilerParams(vmem_limit_bytes=VMEM),
        cost_estimate=pl.CostEstimate(flops=SPAN * 2 * ROWS * 256 * HALF, bytes_accessed=2 * (TOK * D + ROWS * HALF), transcendentals=0),
        name="pick",
    )(micro, caps, routes, x, x)


def pick_again_kernel(pick_ref, lo_ref, hi_ref, out_ref):
    rows = jnp.concatenate([lo_ref[...], hi_ref[...]], axis=0)
    out_ref[...] = jnp.dot(pick_ref[...], rows, preferred_element_type=F32).astype(BF16)


def pick_again(picker, x):
    tile = HALF // 2
    return pl.pallas_call(
        pick_again_kernel,
        out_shape=jax.ShapeDtypeStruct((ROWS, HALF), BF16),
        grid=(2,),
        in_specs=[
            pl.BlockSpec((ROWS, 2 * TOK), lambda i: (0, 0)),
            pl.BlockSpec((TOK, tile), lambda i: (0, i)),
            pl.BlockSpec((TOK, tile), lambda i: (0, i + 2)),
        ],
        out_specs=pl.BlockSpec((ROWS, tile), lambda i: (0, i)),
        compiler_params=pltpu.CompilerParams(vmem_limit_bytes=VMEM),
        cost_estimate=pl.CostEstimate(flops=SPAN * 2 * ROWS * 256 * HALF, bytes_accessed=2 * (TOK * D + ROWS * HALF), transcendentals=0),
        name="pick_again",
    )(picker, x, x)


TOTAL = RING * ROWS
PACK = TOTAL // MSG * 16
RECEIVED = (ROWS, ROWS, ROWS, ROWS // 2, ROWS // 2)


def unpack_rows(refs):
    if len(refs) == 1:
        refs = [refs[0][:, p * MSG : p * MSG + MSG].astype(F32).reshape(ROWS, -1) for p in range(RING)]
    else:
        refs = [r[...].astype(F32) for r in refs]
    x = jnp.concatenate(refs, axis=0)
    x = x.reshape(TOTAL // MSG, 3, 8, x.shape[1])
    lo = jnp.concatenate([x[:, 0:1], x[:, 2:3]], axis=1).reshape(PACK, x.shape[3])
    hi = jnp.concatenate([x[:, 1:2], x[:, 2:3]], axis=1).reshape(PACK, x.shape[3])
    return lo.astype(BF16), hi.astype(BF16)


def pack_rows(lo, hi, outs):
    n = lo.shape[1]
    lo = lo.reshape(TOTAL // MSG, 2, 8, n)
    hi = hi.reshape(TOTAL // MSG, 2, 8, n)
    upper = lax.broadcasted_iota(jnp.int32, (TOTAL // MSG, 1, 8, n), 2) < 4
    last = jnp.where(upper, lo[:, 1:2], hi[:, 1:2])
    tile = jnp.concatenate([lo[:, 0:1], hi[:, 0:1], last], axis=1).reshape(TOTAL, n).astype(BF16)
    at = 0
    for o in outs:
        o[...] = tile[at : at + o.shape[0]]
        at += o.shape[0]


def both_halves(lo, hi):
    lo = lo.reshape(TOTAL // MSG, 2, 8, FF)
    hi = hi.reshape(TOTAL // MSG, 2, 8, FF)
    upper = lax.broadcasted_iota(jnp.int32, (TOTAL // MSG, 8, FF), 1) < 4
    last = jnp.where(upper, lo[:, 1], hi[:, 1])
    last = last + jnp.concatenate([last[:, 4:], last[:, :4]], axis=1)
    return jnp.concatenate([(lo[:, 0] + hi[:, 0])[:, None], last[:, None]], axis=1).reshape(PACK, FF)


def accumulate(i, acc, parts):
    @pl.when(i == 0)
    def _():
        for n, part in enumerate(parts):
            acc[n] = part

    @pl.when(i > 0)
    def _():
        for n, part in enumerate(parts):
            acc[n] += part


def gate_up_step(i, rows, g_lo, g_hi, u_lo, u_hi, acc):
    lo, hi = rows
    dot = lambda x, w: jnp.dot(x, w[...], preferred_element_type=F32)
    accumulate(i, acc, (dot(lo, g_lo), dot(hi, g_hi), dot(lo, u_lo), dot(hi, u_hi)))


def gate_up(acc):
    return both_halves(acc[0], acc[1]), both_halves(acc[2], acc[3])


def saved_kernel(*refs):
    xs, (g_lo, g_hi, u_lo, u_hi, gate_ref, up_ref, acc) = refs[:-7], refs[-7:]
    i = pl.program_id(0)
    for n in range(STEPS):

        @pl.when(i == n)
        def _():
            gate_up_step(i, unpack_rows(xs[:1] if n == 0 else xs[1:]), g_lo, g_hi, u_lo, u_hi, acc)

    @pl.when(i == STEPS - 1)
    def _():
        gate, up = gate_up(acc)
        gate_ref[...] = gate
        up_ref[...] = up


def row_specs(pieces):
    return [pl.BlockSpec((n, TILE), lambda i: (0, jnp.minimum(i, STEPS - 1))) for n in pieces]


def saved_side(xs, gate_w, up_w):
    w = [pl.BlockSpec((TILE, FF), lambda i, k=k: (i + k * STEPS, 0)) for k in (0, 1, 0, 1)]
    return pl.pallas_call(
        saved_kernel,
        out_shape=(jax.ShapeDtypeStruct((PACK, FF), F32),) * 2,
        grid=(STEPS,),
        in_specs=[pl.BlockSpec(x.shape, lambda i, n=x.ndim: (0,) * n) for x in xs] + w,
        out_specs=(pl.BlockSpec((PACK, FF), lambda i: (0, 0)),) * 2,
        scratch_shapes=[pltpu.VMEM((4, PACK, FF), F32)],
        compiler_params=pltpu.CompilerParams(vmem_limit_bytes=VMEM),
        cost_estimate=pl.CostEstimate(
            flops=SPAN * 8 * PACK * HALF * FF, bytes_accessed=2 * (TOTAL * HALF + 2 * D * FF), transcendentals=0
        ),
        name="saved_side",
    )(*xs, gate_w, gate_w, up_w, up_w)


def forward_kernel(x0, x1, x2, x3, x4, g_lo, g_hi, u_lo, u_hi, w_lo, w_hi, o0, o1, o2, o3, o4, acc, mid):
    i = pl.program_id(0)

    @pl.when(i < STEPS)
    def _():
        gate_up_step(i, unpack_rows((x0, x1, x2, x3, x4)), g_lo, g_hi, u_lo, u_hi, acc)

    @pl.when(i == STEPS - 1)
    def _():
        gate, up = gate_up(acc)
        mid[...] = (gate / (1.0 + jnp.exp(-gate)) * up).astype(BF16)

    @pl.when(i >= STEPS)
    def _():
        lo = jnp.dot(mid[...], w_lo[...], preferred_element_type=F32)
        hi = jnp.dot(mid[...], w_hi[...], preferred_element_type=F32)
        pack_rows(lo, hi, (o0, o1, o2, o3, o4))


def forward_side(xs, gate_w, up_w, down_w):
    first = lambda i: jnp.minimum(i, STEPS - 1)
    second = lambda i: jnp.maximum(i - STEPS, 0)
    w = [pl.BlockSpec((TILE, FF), lambda i, k=k: (first(i) + k * STEPS, 0)) for k in (0, 1, 0, 1)]
    w += [pl.BlockSpec((FF, TILE), lambda i, k=k: (0, second(i) + k * STEPS)) for k in (0, 1)]
    return pl.pallas_call(
        forward_kernel,
        out_shape=tuple(jax.ShapeDtypeStruct((n, HALF), BF16) for n in RECEIVED),
        grid=(2 * STEPS,),
        in_specs=row_specs(RECEIVED) + w,
        out_specs=tuple(pl.BlockSpec((n, TILE), lambda i: (0, second(i))) for n in RECEIVED),
        scratch_shapes=[pltpu.VMEM((4, PACK, FF), F32), pltpu.VMEM((PACK, FF), BF16)],
        compiler_params=pltpu.CompilerParams(vmem_limit_bytes=VMEM),
        cost_estimate=pl.CostEstimate(
            flops=SPAN * 12 * PACK * HALF * FF, bytes_accessed=2 * (2 * TOTAL * HALF + 3 * D * FF), transcendentals=PACK * FF
        ),
        name="forward_side",
    )(*xs, gate_w, gate_w, up_w, up_w, down_w, down_w)


def backward_kernel(x0, x1, x2, x3, x4, w_lo, w_hi, gate_ref, up_ref, g_lo, g_hi, u_lo, u_hi, *refs):
    outs, (acc, mid) = refs[:-2], refs[-2:]
    i = pl.program_id(0)
    dot = lambda x, w: lax.dot_general(x, w[...], NT, preferred_element_type=F32)

    @pl.when(i < STEPS)
    def _():
        lo, hi = unpack_rows((x0, x1, x2, x3, x4))
        accumulate(i, acc, (dot(lo, w_lo), dot(hi, w_hi)))

    @pl.when(i == STEPS - 1)
    def _():
        dh = both_halves(acc[0], acc[1])
        gate, up = gate_ref[...], up_ref[...]
        sg = 1.0 / (1.0 + jnp.exp(-gate))
        mid[0] = (dh * up * sg * (1.0 + gate * (1.0 - sg))).astype(BF16)
        mid[1] = (dh * gate * sg).astype(BF16)

    @pl.when(i >= STEPS)
    def _():
        lo = dot(mid[0], g_lo) + dot(mid[1], u_lo)
        hi = dot(mid[0], g_hi) + dot(mid[1], u_hi)
        pack_rows(lo, hi, outs)


def backward_side(xs, gate, up, gate_w, up_w, down_w):
    first = lambda i: jnp.minimum(i, STEPS - 1)
    second = lambda i: jnp.maximum(i - STEPS, 0)
    w = [pl.BlockSpec((FF, TILE), lambda i, k=k: (0, first(i) + k * STEPS)) for k in (0, 1)]
    w += [pl.BlockSpec((PACK, FF), lambda i: (0, 0))] * 2
    w += [pl.BlockSpec((TILE, FF), lambda i, k=k: (second(i) + k * STEPS, 0)) for k in (0, 1, 0, 1)]
    return pl.pallas_call(
        backward_kernel,
        out_shape=tuple(jax.ShapeDtypeStruct((n, HALF), BF16) for n in RECEIVED),
        grid=(2 * STEPS,),
        in_specs=row_specs(RECEIVED) + w,
        out_specs=tuple(pl.BlockSpec((n, TILE), lambda i: (0, second(i))) for n in RECEIVED),
        scratch_shapes=[pltpu.VMEM((2, PACK, FF), F32), pltpu.VMEM((2, PACK, FF), BF16)],
        compiler_params=pltpu.CompilerParams(vmem_limit_bytes=VMEM),
        cost_estimate=pl.CostEstimate(
            flops=SPAN * 12 * PACK * HALF * FF, bytes_accessed=2 * (2 * TOTAL * HALF + 3 * D * FF), transcendentals=PACK * FF
        ),
        name="backward_side",
    )(*xs, down_w, down_w, gate, up, gate_w, gate_w, up_w, up_w)


def spread_kernel(sel_ref, caps_ref, routes_ref, probs_ref, spread_ref, prob_ref):
    routes = routes_ref[0]
    rank = kept_ranks(routes, caps_ref)
    eye = lax.broadcasted_iota(jnp.int32, (TOK, TOK), 0) == lax.broadcasted_iota(jnp.int32, (TOK, TOK), 1)
    column = lambda row: jnp.sum(jnp.where(eye, row, 0.0), axis=1, keepdims=True)
    route_col = column(routes.astype(F32)).astype(jnp.int32)
    rank_col = column(rank.astype(F32)).astype(jnp.int32)
    prob_ref[...] = jnp.broadcast_to(column(probs_ref[0]), (TOK, TOK))
    lane = lax.broadcasted_iota(jnp.int32, (TOK, ROWS), 1)
    expert = (lane * 2731) >> 16
    slot, half = slot_and_half(lane - expert * MSG)
    hit = (route_col == expert) & (rank_col == slot)
    spread_ref[0] = jnp.where(hit & ~half, 1.0, 0.0).astype(BF16)
    spread_ref[1] = jnp.where(hit & half, 1.0, 0.0).astype(BF16)


def spread(micro, caps, routes, probs):
    return pl.pallas_call(
        spread_kernel,
        out_shape=(jax.ShapeDtypeStruct((2, TOK, ROWS), BF16), jax.ShapeDtypeStruct((TOK, TOK), F32)),
        grid_spec=pltpu.PrefetchScalarGridSpec(
            num_scalar_prefetch=2,
            grid=(1,),
            in_specs=[pl.BlockSpec((1, 1, TOK), lambda i, s, c: (s[0], 0, 0))] * 2,
            out_specs=(
                pl.BlockSpec((2, TOK, ROWS), lambda i, s, c: (0, 0, 0)),
                pl.BlockSpec((TOK, TOK), lambda i, s, c: (0, 0)),
            ),
        ),
        name="spread",
    )(micro, caps, routes, probs)


def mix_kernel(count, spread_ref, prob_ref, x_ref, *refs):
    total = refs[0][...]
    if count > 1:
        total = sum(r[...].astype(F32) for r in refs[:count]).astype(BF16)
    found = jnp.dot(spread_ref[0], total, preferred_element_type=F32)
    refs[-1][...] = (x_ref[...].astype(F32) + prob_ref[:, :1] * found).astype(BF16)


def mix(plan, parts, x, first=0, into=None):
    tiles = parts[0].shape[1] // TILE
    into = () if into is None else (into,)
    return pl.pallas_call(
        functools.partial(mix_kernel, len(parts)),
        out_shape=jax.ShapeDtypeStruct((TOK, D), BF16),
        grid=(tiles, 2),
        in_specs=[
            pl.BlockSpec((1, TOK, ROWS), lambda n, h: (h, 0, 0)),
            pl.BlockSpec((TOK, TOK), lambda n, h: (0, 0)),
            pl.BlockSpec((TOK, TILE), lambda n, h: (0, h * STEPS + first + n)),
        ]
        + [pl.BlockSpec((ROWS, TILE), lambda n, h: (0, n)) for _ in parts]
        + [pl.BlockSpec(memory_space=pl.ANY) for _ in into],
        out_specs=pl.BlockSpec((TOK, TILE), lambda n, h: (0, h * STEPS + first + n)),
        input_output_aliases={3 + len(parts): 0} if into else {},
        compiler_params=pltpu.CompilerParams(vmem_limit_bytes=VMEM),
        cost_estimate=pl.CostEstimate(
            flops=SPAN * 4 * ROWS * TOK * TILE * tiles, bytes_accessed=2 * (4 * TOK + ROWS) * TILE * tiles, transcendentals=0
        ),
        name="mix",
    )(*plan, x, *parts, *into)


def shift(x, axis, by):
    n = lax.axis_size(axis)
    return lax.ppermute(x, axis, [(i, (i + by) % n) for i in range(n)])


def labelled(f):
    def call(name, *args):
        with jax.named_scope(name):
            return f(*args)

    return call


@labelled
def exchange(x):
    return lax.all_to_all(x, ("y", "xh"), 0, 0, tiled=True)


@labelled
def gather_ring(x, *first):
    left = shift(x, "z", 1)
    right = shift(x, "z", -1)
    if first:
        left, right, _ = lax.optimization_barrier((left, right, first))
    half = ROWS // 2
    return x, left, right, shift(left[:half], "z", 1), shift(right[half:], "z", -1)


def add(*terms):
    return sum(t.astype(F32) for t in terms).astype(BF16)


def after(x, *others):
    return lax.optimization_barrier((x, others))[0]


@labelled
def scatter_far(far_lo, far_hi):
    return shift(far_lo, "z", 1), shift(far_hi, "z", -1)


def near_kernel(left_ref, right_ref, lo_ref, hi_ref, right_out, left_out):
    half = ROWS // 2
    right_out[:half] = (right_ref[:half].astype(F32) + lo_ref[...].astype(F32)).astype(BF16)
    right_out[half:] = right_ref[half:]
    left_out[:half] = left_ref[:half]
    left_out[half:] = (left_ref[half:].astype(F32) + hi_ref[...].astype(F32)).astype(BF16)


@labelled
def scatter_near(left, right, far):
    spec = lambda n: pl.BlockSpec((n, TILE), lambda i: (0, i))
    right, left = pl.pallas_call(
        near_kernel,
        out_shape=(jax.ShapeDtypeStruct(left.shape, BF16),) * 2,
        grid=(left.shape[1] // TILE,),
        in_specs=[spec(ROWS), spec(ROWS), spec(ROWS // 2), spec(ROWS // 2)],
        out_specs=(spec(ROWS),) * 2,
        compiler_params=pltpu.CompilerParams(vmem_limit_bytes=VMEM),
        cost_estimate=pl.CostEstimate(flops=NEAR * 10**6, bytes_accessed=10 * left.size, transcendentals=0),
        name="near",
    )(left, right, *far)
    return shift(right, "z", 1), shift(left, "z", -1)


def body(
    fwd_boundary,
    grad_boundary,
    saved_inputs,
    routes,
    route_probs,
    capacity,
    roster,
    gate_weight,
    up_weight,
    down_weight,
):
    section = lax.axis_index("pipe")
    sections = lax.axis_size("pipe")
    after_ = (section + 1) % sections
    before = (section + sections - 1) % sections
    take = lambda stack, index: lax.dynamic_index_in_dim(stack, index, 0, keepdims=False)
    fwd_micro = roster[section, 0].reshape(1)
    bwd_micro = roster[section, 1].reshape(1)
    caps = capacity[0]
    route_rows = routes.reshape(2, 1, TOK)
    prob_rows = route_probs.reshape(2, 1, TOK)
    gate_w, up_w, down_w = gate_weight[0, 0], up_weight[0, 0], down_weight[0, 0]

    outgoing = take(fwd_boundary[0], roster[after_, 0])
    layer_input = shift(outgoing, "pipe", 1)
    saved_a, saved_b, bwd_pick = pick(after(bwd_micro, outgoing), caps, route_rows, saved_inputs[0], True)
    own, left, right, far_lo, far_hi = gather_ring("saved_ring_a", saved_a)
    plane_b = exchange("saved_plane_b", saved_b)
    fwd_rows, _ = pick(fwd_micro, caps, route_rows, after(layer_input, plane_b, left, right)[None], False)
    kept_b = gather_ring("saved_ring_b", plane_b)
    _, left_b, right_b, lo_b, hi_b = kept_b
    back_index, fwd_rows, far_lo, far_hi = lax.optimization_barrier((roster[before, 1], fwd_rows, far_lo, far_hi))
    kept_b = (plane_b, left_b, right_b, lo_b, hi_b)
    grad_input = shift(take(grad_boundary[0], back_index), "pipe", -1)
    input_plane = exchange("input_plane", fwd_rows)
    grad_rows = pick_again(bwd_pick, after(grad_input, fwd_rows, kept_b[1], kept_b[2], far_lo, far_hi))
    grad_plane = exchange("grad_plane", grad_rows)
    wide = jnp.stack([own, left, right, jnp.concatenate([far_lo, far_hi], axis=0)]).reshape(RING, EXPERTS, MSG, TILE)
    wide = wide.transpose(1, 0, 2, 3).reshape(EXPERTS, RING * MSG, TILE)
    kept_a = exchange("saved_plane_a", after(wide, grad_plane))
    gate, up = saved_side((kept_a, *kept_b), gate_w, up_w)
    fwd = gather_ring("input_ring", input_plane, grad_plane)
    own, left, right, far_lo, far_hi = forward_side(fwd, gate_w, up_w, down_w)
    far = scatter_far("output_far", far_lo, far_hi)
    grad = gather_ring("grad_ring", grad_plane, own, gate)
    gate, late_routes = lax.optimization_barrier((gate, route_rows))
    parts = backward_side(grad, gate, up, gate_w, up_w, down_w)
    near = scatter_near("output_near", left, right, far)
    fwd_total = exchange("output_plane", add(own, *near))
    far = scatter_far("back_far", *parts[3:])
    near = scatter_near("back_near", *parts[1:3], far)
    bwd_total = exchange("back_plane", add(parts[0], *near))

    fwd_plan = spread(fwd_micro, caps, late_routes, prob_rows)
    bwd_plan = spread(bwd_micro, caps, late_routes, prob_rows)
    new_output = mix(fwd_plan, (fwd_total,), layer_input)
    new_grad = mix(bwd_plan, (bwd_total,), grad_input)
    return new_output[None], new_grad[None]


def solution(mesh):
    grid = Mesh(mesh.devices.reshape(4, 4, 2, 4), ("pipe", "y", "xh", "z"))
    expert = ("y", "xh", "z")
    rows = P("pipe", None, expert, None)
    weight = P("pipe", expert, None, None)
    in_specs = (rows,) * 5 + (P("pipe", None), P()) + (weight,) * 3
    out_specs = (P("pipe", expert, None),) * 2
    return jax.shard_map(body, mesh=grid, in_specs=in_specs, out_specs=out_specs, check_vma=False)
```

```python
import functools

import jax
import jax.numpy as jnp
from jax import lax
from jax.experimental import pallas as pl
from jax.experimental.pallas import tpu as pltpu
from jax.sharding import Mesh, PartitionSpec as P

CAP = 12
EXPERTS = 8
RING = 4
TOK = 128
D = 7168
HALF = D // 2
FF = 256
MSG = 2 * CAP
ROWS = EXPERTS * MSG
TILE = 1792
STEPS = HALF // TILE
SLICE = 3584
NEAR = 10**6
F32 = jnp.float32
BF16 = jnp.bfloat16
NT = (((1,), (1,)), ((), ()))
VMEM = 50 * 2**20
SPAN = 1000


def slot_and_half(r):
    half = ((r >= 8) & (r < 16)) | (r >= 20)
    slot = jnp.where(r < 16, r & 7, 8 + (r & 3))
    return slot, half


def kept_ranks(routes, caps_ref):
    experts = lax.broadcasted_iota(jnp.int32, (EXPERTS, TOK), 0)
    onehot = (routes == experts).astype(F32)
    before = lax.broadcasted_iota(jnp.int32, (TOK, TOK), 0) < lax.broadcasted_iota(jnp.int32, (TOK, TOK), 1)
    earlier = jnp.dot(onehot.astype(BF16), before.astype(F32).astype(BF16), preferred_element_type=F32)
    rank = jnp.sum(onehot * earlier, axis=0, keepdims=True).astype(jnp.int32)
    bound = jnp.zeros((1, TOK), jnp.int32)
    for e in range(EXPERTS):
        bound = jnp.where(routes == e, caps_ref[e], bound)
    return jnp.where(rank < bound, rank, 99)


def pick_kernel(sel_ref, caps_ref, routes_ref, lo_ref, hi_ref, *refs):
    outs, pick_ref = refs[:-1], refs[-1]
    i = pl.program_id(0)

    @pl.when(i == 0)
    def _():
        routes = routes_ref[0]
        rank = kept_ranks(routes, caps_ref)
        shape = (EXPERTS, MSG, TOK)
        expert = lax.broadcasted_iota(jnp.int32, shape, 0)
        slot, half = slot_and_half(lax.broadcasted_iota(jnp.int32, shape, 1))
        hit = (routes[None] == expert) & (rank[None] == slot)
        lo = jnp.where(hit & ~half, 1.0, 0.0).reshape(ROWS, TOK)
        hi = jnp.where(hit & half, 1.0, 0.0).reshape(ROWS, TOK)
        pick_ref[...] = jnp.concatenate([lo, hi], axis=1).astype(BF16)

    rows = jnp.concatenate([lo_ref[0], hi_ref[0]], axis=0)
    tile = jnp.dot(pick_ref[...], rows, preferred_element_type=F32).astype(BF16)
    if len(outs) == 1:
        outs[0][...] = tile
    else:
        for n, out in enumerate(outs):

            @pl.when(i == n)
            def _():
                out[...] = tile


def pick(micro, caps, routes, x, cut):
    own = x.shape[0] > 1
    if cut:
        shapes = [jax.ShapeDtypeStruct((ROWS, TILE), BF16)] * STEPS
        specs = [pl.BlockSpec((ROWS, TILE), lambda i, s, c: (0, 0))] * STEPS
    else:
        shapes = [jax.ShapeDtypeStruct((ROWS, HALF), BF16)]
        specs = [pl.BlockSpec((ROWS, TILE), lambda i, s, c: (0, i))]
    return pl.pallas_call(
        pick_kernel,
        out_shape=shapes + [jax.ShapeDtypeStruct((ROWS, 2 * TOK), BF16)],
        grid_spec=pltpu.PrefetchScalarGridSpec(
            num_scalar_prefetch=2,
            grid=(STEPS,),
            in_specs=[
                pl.BlockSpec((1, 1, TOK), lambda i, s, c: (s[0], 0, 0)),
                pl.BlockSpec((1, TOK, TILE), lambda i, s, c: (s[0] if own else 0, 0, i)),
                pl.BlockSpec((1, TOK, TILE), lambda i, s, c: (s[0] if own else 0, 0, i + STEPS)),
            ],
            out_specs=specs + [pl.BlockSpec((ROWS, 2 * TOK), lambda i, s, c: (0, 0))],
        ),
        compiler_params=pltpu.CompilerParams(vmem_limit_bytes=VMEM),
        cost_estimate=pl.CostEstimate(flops=SPAN * 2 * ROWS * 256 * HALF, bytes_accessed=2 * (TOK * D + ROWS * HALF), transcendentals=0),
        name="pick",
    )(micro, caps, routes, x, x)


def pick_again_kernel(pick_ref, lo_ref, hi_ref, out_ref):
    rows = jnp.concatenate([lo_ref[...], hi_ref[...]], axis=0)
    out_ref[...] = jnp.dot(pick_ref[...], rows, preferred_element_type=F32).astype(BF16)


def pick_again(picker, x):
    tile = HALF // 2
    return pl.pallas_call(
        pick_again_kernel,
        out_shape=jax.ShapeDtypeStruct((ROWS, HALF), BF16),
        grid=(2,),
        in_specs=[
            pl.BlockSpec((ROWS, 2 * TOK), lambda i: (0, 0)),
            pl.BlockSpec((TOK, tile), lambda i: (0, i)),
            pl.BlockSpec((TOK, tile), lambda i: (0, i + 2)),
        ],
        out_specs=pl.BlockSpec((ROWS, tile), lambda i: (0, i)),
        compiler_params=pltpu.CompilerParams(vmem_limit_bytes=VMEM),
        cost_estimate=pl.CostEstimate(flops=SPAN * 2 * ROWS * 256 * HALF, bytes_accessed=2 * (TOK * D + ROWS * HALF), transcendentals=0),
        name="pick_again",
    )(picker, x, x)


TOTAL = RING * ROWS
PACK = TOTAL // MSG * 16
RECEIVED = (ROWS, ROWS, ROWS, ROWS // 2, ROWS // 2)


def unpack_rows(refs):
    if len(refs) == 1:
        refs = [refs[0][:, p * MSG : p * MSG + MSG].astype(F32).reshape(ROWS, -1) for p in range(RING)]
    else:
        refs = [r[...].astype(F32) for r in refs]
    x = jnp.concatenate(refs, axis=0)
    x = x.reshape(TOTAL // MSG, 3, 8, x.shape[1])
    lo = jnp.concatenate([x[:, 0:1], x[:, 2:3]], axis=1).reshape(PACK, x.shape[3])
    hi = jnp.concatenate([x[:, 1:2], x[:, 2:3]], axis=1).reshape(PACK, x.shape[3])
    return lo.astype(BF16), hi.astype(BF16)


def pack_rows(lo, hi, outs):
    n = lo.shape[1]
    lo = lo.reshape(TOTAL // MSG, 2, 8, n)
    hi = hi.reshape(TOTAL // MSG, 2, 8, n)
    upper = lax.broadcasted_iota(jnp.int32, (TOTAL // MSG, 1, 8, n), 2) < 4
    last = jnp.where(upper, lo[:, 1:2], hi[:, 1:2])
    tile = jnp.concatenate([lo[:, 0:1], hi[:, 0:1], last], axis=1).reshape(TOTAL, n).astype(BF16)
    at = 0
    for o in outs:
        o[...] = tile[at : at + o.shape[0]]
        at += o.shape[0]


def both_halves(lo, hi):
    lo = lo.reshape(TOTAL // MSG, 2, 8, FF)
    hi = hi.reshape(TOTAL // MSG, 2, 8, FF)
    upper = lax.broadcasted_iota(jnp.int32, (TOTAL // MSG, 8, FF), 1) < 4
    last = jnp.where(upper, lo[:, 1], hi[:, 1])
    last = last + jnp.concatenate([last[:, 4:], last[:, :4]], axis=1)
    return jnp.concatenate([(lo[:, 0] + hi[:, 0])[:, None], last[:, None]], axis=1).reshape(PACK, FF)


def accumulate(i, acc, parts):
    @pl.when(i == 0)
    def _():
        for n, part in enumerate(parts):
            acc[n] = part

    @pl.when(i > 0)
    def _():
        for n, part in enumerate(parts):
            acc[n] += part


def gate_up_step(i, rows, g_lo, g_hi, u_lo, u_hi, acc):
    lo, hi = rows
    dot = lambda x, w: jnp.dot(x, w[...], preferred_element_type=F32)
    accumulate(i, acc, (dot(lo, g_lo), dot(hi, g_hi), dot(lo, u_lo), dot(hi, u_hi)))


def gate_up(acc):
    return both_halves(acc[0], acc[1]), both_halves(acc[2], acc[3])


def saved_kernel(*refs):
    xs, (g_lo, g_hi, u_lo, u_hi, gate_ref, up_ref, acc) = refs[:-7], refs[-7:]
    i = pl.program_id(0)
    for n in range(STEPS):

        @pl.when(i == n)
        def _():
            gate_up_step(i, unpack_rows(xs[:1] if n == 0 else xs[1:]), g_lo, g_hi, u_lo, u_hi, acc)

    @pl.when(i == STEPS - 1)
    def _():
        gate, up = gate_up(acc)
        gate_ref[...] = gate
        up_ref[...] = up


def row_specs(pieces):
    return [pl.BlockSpec((n, TILE), lambda i: (0, jnp.minimum(i, STEPS - 1))) for n in pieces]


def saved_side(xs, gate_w, up_w):
    w = [pl.BlockSpec((TILE, FF), lambda i, k=k: (i + k * STEPS, 0)) for k in (0, 1, 0, 1)]
    return pl.pallas_call(
        saved_kernel,
        out_shape=(jax.ShapeDtypeStruct((PACK, FF), F32),) * 2,
        grid=(STEPS,),
        in_specs=[pl.BlockSpec(x.shape, lambda i, n=x.ndim: (0,) * n) for x in xs] + w,
        out_specs=(pl.BlockSpec((PACK, FF), lambda i: (0, 0)),) * 2,
        scratch_shapes=[pltpu.VMEM((4, PACK, FF), F32)],
        compiler_params=pltpu.CompilerParams(vmem_limit_bytes=VMEM),
        cost_estimate=pl.CostEstimate(
            flops=SPAN * 8 * PACK * HALF * FF, bytes_accessed=2 * (TOTAL * HALF + 2 * D * FF), transcendentals=0
        ),
        name="saved_side",
    )(*xs, gate_w, gate_w, up_w, up_w)


def forward_kernel(x0, x1, x2, x3, x4, g_lo, g_hi, u_lo, u_hi, w_lo, w_hi, o0, o1, o2, o3, o4, acc, mid):
    i = pl.program_id(0)

    @pl.when(i < STEPS)
    def _():
        gate_up_step(i, unpack_rows((x0, x1, x2, x3, x4)), g_lo, g_hi, u_lo, u_hi, acc)

    @pl.when(i == STEPS - 1)
    def _():
        gate, up = gate_up(acc)
        mid[...] = (gate / (1.0 + jnp.exp(-gate)) * up).astype(BF16)

    @pl.when(i >= STEPS)
    def _():
        lo = jnp.dot(mid[...], w_lo[...], preferred_element_type=F32)
        hi = jnp.dot(mid[...], w_hi[...], preferred_element_type=F32)
        pack_rows(lo, hi, (o0, o1, o2, o3, o4))


def forward_side(xs, gate_w, up_w, down_w):
    first = lambda i: jnp.minimum(i, STEPS - 1)
    second = lambda i: jnp.maximum(i - STEPS, 0)
    w = [pl.BlockSpec((TILE, FF), lambda i, k=k: (first(i) + k * STEPS, 0)) for k in (0, 1, 0, 1)]
    w += [pl.BlockSpec((FF, TILE), lambda i, k=k: (0, second(i) + k * STEPS)) for k in (0, 1)]
    return pl.pallas_call(
        forward_kernel,
        out_shape=tuple(jax.ShapeDtypeStruct((n, HALF), BF16) for n in RECEIVED),
        grid=(2 * STEPS,),
        in_specs=row_specs(RECEIVED) + w,
        out_specs=tuple(pl.BlockSpec((n, TILE), lambda i: (0, second(i))) for n in RECEIVED),
        scratch_shapes=[pltpu.VMEM((4, PACK, FF), F32), pltpu.VMEM((PACK, FF), BF16)],
        compiler_params=pltpu.CompilerParams(vmem_limit_bytes=VMEM),
        cost_estimate=pl.CostEstimate(
            flops=SPAN * 12 * PACK * HALF * FF, bytes_accessed=2 * (2 * TOTAL * HALF + 3 * D * FF), transcendentals=PACK * FF
        ),
        name="forward_side",
    )(*xs, gate_w, gate_w, up_w, up_w, down_w, down_w)


def backward_kernel(x0, x1, x2, x3, x4, w_lo, w_hi, gate_ref, up_ref, g_lo, g_hi, u_lo, u_hi, *refs):
    outs, (acc, mid) = refs[:-2], refs[-2:]
    i = pl.program_id(0)
    dot = lambda x, w: lax.dot_general(x, w[...], NT, preferred_element_type=F32)

    @pl.when(i < STEPS)
    def _():
        lo, hi = unpack_rows((x0, x1, x2, x3, x4))
        accumulate(i, acc, (dot(lo, w_lo), dot(hi, w_hi)))

    @pl.when(i == STEPS - 1)
    def _():
        dh = both_halves(acc[0], acc[1])
        gate, up = gate_ref[...], up_ref[...]
        sg = 1.0 / (1.0 + jnp.exp(-gate))
        mid[0] = (dh * up * sg * (1.0 + gate * (1.0 - sg))).astype(BF16)
        mid[1] = (dh * gate * sg).astype(BF16)

    @pl.when(i >= STEPS)
    def _():
        lo = dot(mid[0], g_lo) + dot(mid[1], u_lo)
        hi = dot(mid[0], g_hi) + dot(mid[1], u_hi)
        pack_rows(lo, hi, outs)


def backward_side(xs, gate, up, gate_w, up_w, down_w):
    first = lambda i: jnp.minimum(i, STEPS - 1)
    second = lambda i: jnp.maximum(i - STEPS, 0)
    w = [pl.BlockSpec((FF, TILE), lambda i, k=k: (0, first(i) + k * STEPS)) for k in (0, 1)]
    w += [pl.BlockSpec((PACK, FF), lambda i: (0, 0))] * 2
    w += [pl.BlockSpec((TILE, FF), lambda i, k=k: (second(i) + k * STEPS, 0)) for k in (0, 1, 0, 1)]
    return pl.pallas_call(
        backward_kernel,
        out_shape=tuple(jax.ShapeDtypeStruct((n, HALF), BF16) for n in RECEIVED),
        grid=(2 * STEPS,),
        in_specs=row_specs(RECEIVED) + w,
        out_specs=tuple(pl.BlockSpec((n, TILE), lambda i: (0, second(i))) for n in RECEIVED),
        scratch_shapes=[pltpu.VMEM((2, PACK, FF), F32), pltpu.VMEM((2, PACK, FF), BF16)],
        compiler_params=pltpu.CompilerParams(vmem_limit_bytes=VMEM),
        cost_estimate=pl.CostEstimate(
            flops=SPAN * 12 * PACK * HALF * FF, bytes_accessed=2 * (2 * TOTAL * HALF + 3 * D * FF), transcendentals=PACK * FF
        ),
        name="backward_side",
    )(*xs, down_w, down_w, gate, up, gate_w, gate_w, up_w, up_w)


def spread_kernel(sel_ref, caps_ref, routes_ref, probs_ref, spread_ref, prob_ref):
    routes = routes_ref[0]
    rank = kept_ranks(routes, caps_ref)
    eye = lax.broadcasted_iota(jnp.int32, (TOK, TOK), 0) == lax.broadcasted_iota(jnp.int32, (TOK, TOK), 1)
    column = lambda row: jnp.sum(jnp.where(eye, row, 0.0), axis=1, keepdims=True)
    route_col = column(routes.astype(F32)).astype(jnp.int32)
    rank_col = column(rank.astype(F32)).astype(jnp.int32)
    prob_ref[...] = jnp.broadcast_to(column(probs_ref[0]), (TOK, TOK))
    lane = lax.broadcasted_iota(jnp.int32, (TOK, ROWS), 1)
    expert = (lane * 2731) >> 16
    slot, half = slot_and_half(lane - expert * MSG)
    hit = (route_col == expert) & (rank_col == slot)
    spread_ref[0] = jnp.where(hit & ~half, 1.0, 0.0).astype(BF16)
    spread_ref[1] = jnp.where(hit & half, 1.0, 0.0).astype(BF16)


def spread(micro, caps, routes, probs):
    return pl.pallas_call(
        spread_kernel,
        out_shape=(jax.ShapeDtypeStruct((2, TOK, ROWS), BF16), jax.ShapeDtypeStruct((TOK, TOK), F32)),
        grid_spec=pltpu.PrefetchScalarGridSpec(
            num_scalar_prefetch=2,
            grid=(1,),
            in_specs=[pl.BlockSpec((1, 1, TOK), lambda i, s, c: (s[0], 0, 0))] * 2,
            out_specs=(
                pl.BlockSpec((2, TOK, ROWS), lambda i, s, c: (0, 0, 0)),
                pl.BlockSpec((TOK, TOK), lambda i, s, c: (0, 0)),
            ),
        ),
        name="spread",
    )(micro, caps, routes, probs)


def mix_kernel(count, spread_ref, prob_ref, x_ref, *refs):
    total = refs[0][...]
    if count > 1:
        total = sum(r[...].astype(F32) for r in refs[:count]).astype(BF16)
    found = jnp.dot(spread_ref[0], total, preferred_element_type=F32)
    refs[-1][...] = (x_ref[...].astype(F32) + prob_ref[:, :1] * found).astype(BF16)


def mix(plan, parts, x, first=0, into=None):
    tiles = parts[0].shape[1] // SLICE
    into = () if into is None else (into,)
    return pl.pallas_call(
        functools.partial(mix_kernel, len(parts)),
        out_shape=jax.ShapeDtypeStruct((TOK, D), BF16),
        grid=(tiles, 2),
        in_specs=[
            pl.BlockSpec((1, TOK, ROWS), lambda n, h: (h, 0, 0)),
            pl.BlockSpec((TOK, TOK), lambda n, h: (0, 0)),
            pl.BlockSpec((TOK, SLICE), lambda n, h: (0, h * (HALF // SLICE) + first + n)),
        ]
        + [pl.BlockSpec((ROWS, SLICE), lambda n, h: (0, n)) for _ in parts]
        + [pl.BlockSpec(memory_space=pl.ANY) for _ in into],
        out_specs=pl.BlockSpec((TOK, SLICE), lambda n, h: (0, h * (HALF // SLICE) + first + n)),
        input_output_aliases={3 + len(parts): 0} if into else {},
        compiler_params=pltpu.CompilerParams(vmem_limit_bytes=VMEM),
        cost_estimate=pl.CostEstimate(
            flops=SPAN * 4 * ROWS * TOK * SLICE * tiles, bytes_accessed=2 * (4 * TOK + ROWS) * SLICE * tiles, transcendentals=0
        ),
        name="mix",
    )(*plan, x, *parts, *into)


def shift(x, axis, by):
    n = lax.axis_size(axis)
    return lax.ppermute(x, axis, [(i, (i + by) % n) for i in range(n)])


def labelled(f):
    def call(name, *args):
        with jax.named_scope(name):
            return f(*args)

    return call


@labelled
def exchange(x):
    return lax.all_to_all(x, ("y", "xh"), 0, 0, tiled=True)


@labelled
def gather_ring(x, *first):
    left = shift(x, "z", 1)
    right = shift(x, "z", -1)
    if first:
        left, right, _ = lax.optimization_barrier((left, right, first))
    half = ROWS // 2
    return x, left, right, shift(left[:half], "z", 1), shift(right[half:], "z", -1)


def add(*terms):
    return sum(t.astype(F32) for t in terms).astype(BF16)


def after(x, *others):
    return lax.optimization_barrier((x, others))[0]


@labelled
def scatter_far(far_lo, far_hi):
    return shift(far_lo, "z", 1), shift(far_hi, "z", -1)


def near_kernel(left_ref, right_ref, lo_ref, hi_ref, right_out, left_out):
    half = ROWS // 2
    right_out[:half] = (right_ref[:half].astype(F32) + lo_ref[...].astype(F32)).astype(BF16)
    right_out[half:] = right_ref[half:]
    left_out[:half] = left_ref[:half]
    left_out[half:] = (left_ref[half:].astype(F32) + hi_ref[...].astype(F32)).astype(BF16)


@labelled
def scatter_near(left, right, far):
    spec = lambda n: pl.BlockSpec((n, TILE), lambda i: (0, i))
    right, left = pl.pallas_call(
        near_kernel,
        out_shape=(jax.ShapeDtypeStruct(left.shape, BF16),) * 2,
        grid=(left.shape[1] // TILE,),
        in_specs=[spec(ROWS), spec(ROWS), spec(ROWS // 2), spec(ROWS // 2)],
        out_specs=(spec(ROWS),) * 2,
        compiler_params=pltpu.CompilerParams(vmem_limit_bytes=VMEM),
        cost_estimate=pl.CostEstimate(flops=NEAR * 10**6, bytes_accessed=10 * left.size, transcendentals=0),
        name="near",
    )(left, right, *far)
    return shift(right, "z", 1), shift(left, "z", -1)


def body(
    fwd_boundary,
    grad_boundary,
    saved_inputs,
    routes,
    route_probs,
    capacity,
    roster,
    gate_weight,
    up_weight,
    down_weight,
):
    section = lax.axis_index("pipe")
    sections = lax.axis_size("pipe")
    after_ = (section + 1) % sections
    before = (section + sections - 1) % sections
    take = lambda stack, index: lax.dynamic_index_in_dim(stack, index, 0, keepdims=False)
    fwd_micro = roster[section, 0].reshape(1)
    bwd_micro = roster[section, 1].reshape(1)
    caps = capacity[0]
    route_rows = routes.reshape(2, 1, TOK)
    prob_rows = route_probs.reshape(2, 1, TOK)
    gate_w, up_w, down_w = gate_weight[0, 0], up_weight[0, 0], down_weight[0, 0]

    outgoing = take(fwd_boundary[0], roster[after_, 0])
    layer_input = shift(outgoing, "pipe", 1)
    saved_a, saved_b, bwd_pick = pick(after(bwd_micro, outgoing), caps, route_rows, saved_inputs[0], True)
    own, left, right, far_lo, far_hi = gather_ring("saved_ring_a", saved_a)
    plane_b = exchange("saved_plane_b", saved_b)
    left, right, back_index = lax.optimization_barrier((left, right, roster[before, 1]))
    fwd_rows, _ = pick(fwd_micro, caps, route_rows, after(layer_input, plane_b, left, right)[None], False)
    kept_b = gather_ring("saved_ring_b", plane_b)
    _, left_b, right_b, lo_b, hi_b = kept_b
    fwd_rows, far_lo, far_hi = lax.optimization_barrier((fwd_rows, far_lo, far_hi))
    kept_b = (plane_b, left_b, right_b, lo_b, hi_b)
    grad_input = shift(take(grad_boundary[0], back_index), "pipe", -1)
    input_plane = exchange("input_plane", fwd_rows)
    grad_rows = pick_again(bwd_pick, after(grad_input, fwd_rows, kept_b[1], kept_b[2], far_lo, far_hi))
    grad_plane = exchange("grad_plane", grad_rows)
    wide = jnp.stack([own, left, right, jnp.concatenate([far_lo, far_hi], axis=0)]).reshape(RING, EXPERTS, MSG, TILE)
    wide = wide.transpose(1, 0, 2, 3).reshape(EXPERTS, RING * MSG, TILE)
    kept_a = exchange("saved_plane_a", after(wide, grad_plane))
    gate, up = saved_side((kept_a, *kept_b), gate_w, up_w)
    fwd = gather_ring("input_ring", input_plane, grad_plane)
    own, left, right, far_lo, far_hi = forward_side(fwd, gate_w, up_w, down_w)
    far = scatter_far("output_far", far_lo, far_hi)
    grad = gather_ring("grad_ring", grad_plane, own, gate)
    gate, late_routes = lax.optimization_barrier((gate, route_rows))
    parts = backward_side(grad, gate, up, gate_w, up_w, down_w)
    near = scatter_near("output_near", left, right, far)
    fwd_total = exchange("output_plane", add(own, *near))
    far = scatter_far("back_far", *parts[3:])
    near = scatter_near("back_near", *parts[1:3], far)
    bwd_total = exchange("back_plane", add(parts[0], *near))

    fwd_plan = spread(fwd_micro, caps, late_routes, prob_rows)
    bwd_plan = spread(bwd_micro, caps, late_routes, prob_rows)
    new_output = mix(fwd_plan, (fwd_total,), layer_input)
    new_grad = mix(bwd_plan, (bwd_total,), grad_input)
    return new_output[None], new_grad[None]


def solution(mesh):
    grid = Mesh(mesh.devices.reshape(4, 4, 2, 4), ("pipe", "y", "xh", "z"))
    expert = ("y", "xh", "z")
    rows = P("pipe", None, expert, None)
    weight = P("pipe", expert, None, None)
    in_specs = (rows,) * 5 + (P("pipe", None), P()) + (weight,) * 3
    out_specs = (P("pipe", expert, None),) * 2
    return jax.shard_map(body, mesh=grid, in_specs=in_specs, out_specs=out_specs, check_vma=False)
```

```python
import functools

import jax
import jax.numpy as jnp
from jax import lax
from jax.experimental import pallas as pl
from jax.experimental.pallas import tpu as pltpu
from jax.sharding import Mesh, PartitionSpec as P

CAP = 12
EXPERTS = 8
RING = 4
TOK = 128
D = 7168
HALF = D // 2
FF = 256
MSG = 2 * CAP
ROWS = EXPERTS * MSG
TILE = 1792
STEPS = HALF // TILE
SLICE = 3584
NEAR = 10**6
F32 = jnp.float32
BF16 = jnp.bfloat16
NT = (((1,), (1,)), ((), ()))
VMEM = 50 * 2**20
SPAN = 1000


def slot_and_half(r):
    half = ((r >= 8) & (r < 16)) | (r >= 20)
    slot = jnp.where(r < 16, r & 7, 8 + (r & 3))
    return slot, half


def kept_ranks(routes, caps_ref):
    experts = lax.broadcasted_iota(jnp.int32, (EXPERTS, TOK), 0)
    onehot = (routes == experts).astype(F32)
    before = lax.broadcasted_iota(jnp.int32, (TOK, TOK), 0) < lax.broadcasted_iota(jnp.int32, (TOK, TOK), 1)
    earlier = jnp.dot(onehot.astype(BF16), before.astype(F32).astype(BF16), preferred_element_type=F32)
    rank = jnp.sum(onehot * earlier, axis=0, keepdims=True).astype(jnp.int32)
    bound = jnp.zeros((1, TOK), jnp.int32)
    for e in range(EXPERTS):
        bound = jnp.where(routes == e, caps_ref[e], bound)
    return jnp.where(rank < bound, rank, 99)


def pick_kernel(sel_ref, caps_ref, routes_ref, lo_ref, hi_ref, *refs):
    outs, pick_ref = refs[:-1], refs[-1]
    i = pl.program_id(0)

    @pl.when(i == 0)
    def _():
        routes = routes_ref[0]
        rank = kept_ranks(routes, caps_ref)
        shape = (EXPERTS, MSG, TOK)
        expert = lax.broadcasted_iota(jnp.int32, shape, 0)
        slot, half = slot_and_half(lax.broadcasted_iota(jnp.int32, shape, 1))
        hit = (routes[None] == expert) & (rank[None] == slot)
        lo = jnp.where(hit & ~half, 1.0, 0.0).reshape(ROWS, TOK)
        hi = jnp.where(hit & half, 1.0, 0.0).reshape(ROWS, TOK)
        pick_ref[...] = jnp.concatenate([lo, hi], axis=1).astype(BF16)

    rows = jnp.concatenate([lo_ref[0], hi_ref[0]], axis=0)
    tile = jnp.dot(pick_ref[...], rows, preferred_element_type=F32).astype(BF16)
    if len(outs) == 1:
        outs[0][...] = tile
    else:
        for n, out in enumerate(outs):

            @pl.when(i == n)
            def _():
                out[...] = tile


def pick(micro, caps, routes, x, cut):
    own = x.shape[0] > 1
    if cut:
        shapes = [jax.ShapeDtypeStruct((ROWS, TILE), BF16)] * STEPS
        specs = [pl.BlockSpec((ROWS, TILE), lambda i, s, c: (0, 0))] * STEPS
    else:
        shapes = [jax.ShapeDtypeStruct((ROWS, HALF), BF16)]
        specs = [pl.BlockSpec((ROWS, TILE), lambda i, s, c: (0, i))]
    return pl.pallas_call(
        pick_kernel,
        out_shape=shapes + [jax.ShapeDtypeStruct((ROWS, 2 * TOK), BF16)],
        grid_spec=pltpu.PrefetchScalarGridSpec(
            num_scalar_prefetch=2,
            grid=(STEPS,),
            in_specs=[
                pl.BlockSpec((1, 1, TOK), lambda i, s, c: (s[0], 0, 0)),
                pl.BlockSpec((1, TOK, TILE), lambda i, s, c: (s[0] if own else 0, 0, i)),
                pl.BlockSpec((1, TOK, TILE), lambda i, s, c: (s[0] if own else 0, 0, i + STEPS)),
            ],
            out_specs=specs + [pl.BlockSpec((ROWS, 2 * TOK), lambda i, s, c: (0, 0))],
        ),
        compiler_params=pltpu.CompilerParams(vmem_limit_bytes=VMEM),
        cost_estimate=pl.CostEstimate(flops=SPAN * 2 * ROWS * 256 * HALF, bytes_accessed=2 * (TOK * D + ROWS * HALF), transcendentals=0),
        name="pick",
    )(micro, caps, routes, x, x)


def pick_again_kernel(pick_ref, lo_ref, hi_ref, out_ref):
    rows = jnp.concatenate([lo_ref[...], hi_ref[...]], axis=0)
    out_ref[...] = jnp.dot(pick_ref[...], rows, preferred_element_type=F32).astype(BF16)


def pick_again(picker, x):
    tile = HALF
    return pl.pallas_call(
        pick_again_kernel,
        out_shape=jax.ShapeDtypeStruct((ROWS, HALF), BF16),
        grid=(1,),
        in_specs=[
            pl.BlockSpec((ROWS, 2 * TOK), lambda i: (0, 0)),
            pl.BlockSpec((TOK, tile), lambda i: (0, i)),
            pl.BlockSpec((TOK, tile), lambda i: (0, i + 1)),
        ],
        out_specs=pl.BlockSpec((ROWS, tile), lambda i: (0, i)),
        compiler_params=pltpu.CompilerParams(vmem_limit_bytes=VMEM),
        cost_estimate=pl.CostEstimate(flops=SPAN * 2 * ROWS * 256 * HALF, bytes_accessed=2 * (TOK * D + ROWS * HALF), transcendentals=0),
        name="pick_again",
    )(picker, x, x)


TOTAL = RING * ROWS
PACK = TOTAL // MSG * 16
RECEIVED = (ROWS, ROWS, ROWS, ROWS // 2, ROWS // 2)


def unpack_rows(refs):
    if len(refs) == 1:
        refs = [refs[0][:, p * MSG : p * MSG + MSG].astype(F32).reshape(ROWS, -1) for p in range(RING)]
    else:
        refs = [r[...].astype(F32) for r in refs]
    x = jnp.concatenate(refs, axis=0)
    x = x.reshape(TOTAL // MSG, 3, 8, x.shape[1])
    lo = jnp.concatenate([x[:, 0:1], x[:, 2:3]], axis=1).reshape(PACK, x.shape[3])
    hi = jnp.concatenate([x[:, 1:2], x[:, 2:3]], axis=1).reshape(PACK, x.shape[3])
    return lo.astype(BF16), hi.astype(BF16)


def pack_rows(lo, hi, outs):
    n = lo.shape[1]
    lo = lo.reshape(TOTAL // MSG, 2, 8, n)
    hi = hi.reshape(TOTAL // MSG, 2, 8, n)
    upper = lax.broadcasted_iota(jnp.int32, (TOTAL // MSG, 1, 8, n), 2) < 4
    last = jnp.where(upper, lo[:, 1:2], hi[:, 1:2])
    tile = jnp.concatenate([lo[:, 0:1], hi[:, 0:1], last], axis=1).reshape(TOTAL, n).astype(BF16)
    at = 0
    for o in outs:
        o[...] = tile[at : at + o.shape[0]]
        at += o.shape[0]


def both_halves(lo, hi):
    lo = lo.reshape(TOTAL // MSG, 2, 8, FF)
    hi = hi.reshape(TOTAL // MSG, 2, 8, FF)
    upper = lax.broadcasted_iota(jnp.int32, (TOTAL // MSG, 8, FF), 1) < 4
    last = jnp.where(upper, lo[:, 1], hi[:, 1])
    last = last + jnp.concatenate([last[:, 4:], last[:, :4]], axis=1)
    return jnp.concatenate([(lo[:, 0] + hi[:, 0])[:, None], last[:, None]], axis=1).reshape(PACK, FF)


def accumulate(i, acc, parts):
    @pl.when(i == 0)
    def _():
        for n, part in enumerate(parts):
            acc[n] = part

    @pl.when(i > 0)
    def _():
        for n, part in enumerate(parts):
            acc[n] += part


def gate_up_step(i, rows, g_lo, g_hi, u_lo, u_hi, acc):
    lo, hi = rows
    dot = lambda x, w: jnp.dot(x, w[...], preferred_element_type=F32)
    accumulate(i, acc, (dot(lo, g_lo), dot(hi, g_hi), dot(lo, u_lo), dot(hi, u_hi)))


def gate_up(acc):
    return both_halves(acc[0], acc[1]), both_halves(acc[2], acc[3])


def saved_kernel(*refs):
    xs, (g_lo, g_hi, u_lo, u_hi, gate_ref, up_ref, acc) = refs[:-7], refs[-7:]
    i = pl.program_id(0)
    for n in range(STEPS):

        @pl.when(i == n)
        def _():
            gate_up_step(i, unpack_rows(xs[:1] if n == 0 else xs[1:]), g_lo, g_hi, u_lo, u_hi, acc)

    @pl.when(i == STEPS - 1)
    def _():
        gate, up = gate_up(acc)
        gate_ref[...] = gate
        up_ref[...] = up


def row_specs(pieces):
    return [pl.BlockSpec((n, TILE), lambda i: (0, jnp.minimum(i, STEPS - 1))) for n in pieces]


def saved_side(xs, gate_w, up_w):
    w = [pl.BlockSpec((TILE, FF), lambda i, k=k: (i + k * STEPS, 0)) for k in (0, 1, 0, 1)]
    return pl.pallas_call(
        saved_kernel,
        out_shape=(jax.ShapeDtypeStruct((PACK, FF), F32),) * 2,
        grid=(STEPS,),
        in_specs=[pl.BlockSpec(x.shape, lambda i, n=x.ndim: (0,) * n) for x in xs] + w,
        out_specs=(pl.BlockSpec((PACK, FF), lambda i: (0, 0)),) * 2,
        scratch_shapes=[pltpu.VMEM((4, PACK, FF), F32)],
        compiler_params=pltpu.CompilerParams(vmem_limit_bytes=VMEM),
        cost_estimate=pl.CostEstimate(
            flops=SPAN * 8 * PACK * HALF * FF, bytes_accessed=2 * (TOTAL * HALF + 2 * D * FF), transcendentals=0
        ),
        name="saved_side",
    )(*xs, gate_w, gate_w, up_w, up_w)


def forward_kernel(x0, x1, x2, x3, x4, g_lo, g_hi, u_lo, u_hi, w_lo, w_hi, o0, o1, o2, o3, o4, acc, mid):
    i = pl.program_id(0)

    @pl.when(i < STEPS)
    def _():
        gate_up_step(i, unpack_rows((x0, x1, x2, x3, x4)), g_lo, g_hi, u_lo, u_hi, acc)

    @pl.when(i == STEPS - 1)
    def _():
        gate, up = gate_up(acc)
        mid[...] = (gate / (1.0 + jnp.exp(-gate)) * up).astype(BF16)

    @pl.when(i >= STEPS)
    def _():
        lo = jnp.dot(mid[...], w_lo[...], preferred_element_type=F32)
        hi = jnp.dot(mid[...], w_hi[...], preferred_element_type=F32)
        pack_rows(lo, hi, (o0, o1, o2, o3, o4))


def forward_side(xs, gate_w, up_w, down_w):
    first = lambda i: jnp.minimum(i, STEPS - 1)
    second = lambda i: jnp.maximum(i - STEPS, 0)
    w = [pl.BlockSpec((TILE, FF), lambda i, k=k: (first(i) + k * STEPS, 0)) for k in (0, 1, 0, 1)]
    w += [pl.BlockSpec((FF, TILE), lambda i, k=k: (0, second(i) + k * STEPS)) for k in (0, 1)]
    return pl.pallas_call(
        forward_kernel,
        out_shape=tuple(jax.ShapeDtypeStruct((n, HALF), BF16) for n in RECEIVED),
        grid=(2 * STEPS,),
        in_specs=row_specs(RECEIVED) + w,
        out_specs=tuple(pl.BlockSpec((n, TILE), lambda i: (0, second(i))) for n in RECEIVED),
        scratch_shapes=[pltpu.VMEM((4, PACK, FF), F32), pltpu.VMEM((PACK, FF), BF16)],
        compiler_params=pltpu.CompilerParams(vmem_limit_bytes=VMEM),
        cost_estimate=pl.CostEstimate(
            flops=SPAN * 12 * PACK * HALF * FF, bytes_accessed=2 * (2 * TOTAL * HALF + 3 * D * FF), transcendentals=PACK * FF
        ),
        name="forward_side",
    )(*xs, gate_w, gate_w, up_w, up_w, down_w, down_w)


def backward_kernel(x0, x1, x2, x3, x4, w_lo, w_hi, gate_ref, up_ref, g_lo, g_hi, u_lo, u_hi, *refs):
    outs, (acc, mid) = refs[:-2], refs[-2:]
    i = pl.program_id(0)
    dot = lambda x, w: lax.dot_general(x, w[...], NT, preferred_element_type=F32)

    @pl.when(i < STEPS)
    def _():
        lo, hi = unpack_rows((x0, x1, x2, x3, x4))
        accumulate(i, acc, (dot(lo, w_lo), dot(hi, w_hi)))

    @pl.when(i == STEPS - 1)
    def _():
        dh = both_halves(acc[0], acc[1])
        gate, up = gate_ref[...], up_ref[...]
        sg = 1.0 / (1.0 + jnp.exp(-gate))
        mid[0] = (dh * up * sg * (1.0 + gate * (1.0 - sg))).astype(BF16)
        mid[1] = (dh * gate * sg).astype(BF16)

    @pl.when(i >= STEPS)
    def _():
        lo = dot(mid[0], g_lo) + dot(mid[1], u_lo)
        hi = dot(mid[0], g_hi) + dot(mid[1], u_hi)
        pack_rows(lo, hi, outs)


def backward_side(xs, gate, up, gate_w, up_w, down_w):
    first = lambda i: jnp.minimum(i, STEPS - 1)
    second = lambda i: jnp.maximum(i - STEPS, 0)
    w = [pl.BlockSpec((FF, TILE), lambda i, k=k: (0, first(i) + k * STEPS)) for k in (0, 1)]
    w += [pl.BlockSpec((PACK, FF), lambda i: (0, 0))] * 2
    w += [pl.BlockSpec((TILE, FF), lambda i, k=k: (second(i) + k * STEPS, 0)) for k in (0, 1, 0, 1)]
    return pl.pallas_call(
        backward_kernel,
        out_shape=tuple(jax.ShapeDtypeStruct((n, HALF), BF16) for n in RECEIVED),
        grid=(2 * STEPS,),
        in_specs=row_specs(RECEIVED) + w,
        out_specs=tuple(pl.BlockSpec((n, TILE), lambda i: (0, second(i))) for n in RECEIVED),
        scratch_shapes=[pltpu.VMEM((2, PACK, FF), F32), pltpu.VMEM((2, PACK, FF), BF16)],
        compiler_params=pltpu.CompilerParams(vmem_limit_bytes=VMEM),
        cost_estimate=pl.CostEstimate(
            flops=SPAN * 12 * PACK * HALF * FF, bytes_accessed=2 * (2 * TOTAL * HALF + 3 * D * FF), transcendentals=PACK * FF
        ),
        name="backward_side",
    )(*xs, down_w, down_w, gate, up, gate_w, gate_w, up_w, up_w)


def spread_kernel(sel_ref, caps_ref, routes_ref, probs_ref, spread_ref, prob_ref):
    routes = routes_ref[0]
    rank = kept_ranks(routes, caps_ref)
    eye = lax.broadcasted_iota(jnp.int32, (TOK, TOK), 0) == lax.broadcasted_iota(jnp.int32, (TOK, TOK), 1)
    column = lambda row: jnp.sum(jnp.where(eye, row, 0.0), axis=1, keepdims=True)
    route_col = column(routes.astype(F32)).astype(jnp.int32)
    rank_col = column(rank.astype(F32)).astype(jnp.int32)
    prob_ref[...] = jnp.broadcast_to(column(probs_ref[0]), (TOK, TOK))
    lane = lax.broadcasted_iota(jnp.int32, (TOK, ROWS), 1)
    expert = (lane * 2731) >> 16
    slot, half = slot_and_half(lane - expert * MSG)
    hit = (route_col == expert) & (rank_col == slot)
    spread_ref[0] = jnp.where(hit & ~half, 1.0, 0.0).astype(BF16)
    spread_ref[1] = jnp.where(hit & half, 1.0, 0.0).astype(BF16)


def spread(micro, caps, routes, probs):
    return pl.pallas_call(
        spread_kernel,
        out_shape=(jax.ShapeDtypeStruct((2, TOK, ROWS), BF16), jax.ShapeDtypeStruct((TOK, TOK), F32)),
        grid_spec=pltpu.PrefetchScalarGridSpec(
            num_scalar_prefetch=2,
            grid=(1,),
            in_specs=[pl.BlockSpec((1, 1, TOK), lambda i, s, c: (s[0], 0, 0))] * 2,
            out_specs=(
                pl.BlockSpec((2, TOK, ROWS), lambda i, s, c: (0, 0, 0)),
                pl.BlockSpec((TOK, TOK), lambda i, s, c: (0, 0)),
            ),
        ),
        name="spread",
    )(micro, caps, routes, probs)


def mix_kernel(count, spread_ref, prob_ref, x_ref, *refs):
    total = refs[0][...]
    if count > 1:
        total = sum(r[...].astype(F32) for r in refs[:count]).astype(BF16)
    found = jnp.dot(spread_ref[0], total, preferred_element_type=F32)
    refs[-1][...] = (x_ref[...].astype(F32) + prob_ref[:, :1] * found).astype(BF16)


def mix(plan, parts, x, first=0, into=None):
    tiles = parts[0].shape[1] // SLICE
    into = () if into is None else (into,)
    return pl.pallas_call(
        functools.partial(mix_kernel, len(parts)),
        out_shape=jax.ShapeDtypeStruct((TOK, D), BF16),
        grid=(tiles, 2),
        in_specs=[
            pl.BlockSpec((1, TOK, ROWS), lambda n, h: (h, 0, 0)),
            pl.BlockSpec((TOK, TOK), lambda n, h: (0, 0)),
            pl.BlockSpec((TOK, SLICE), lambda n, h: (0, h * (HALF // SLICE) + first + n)),
        ]
        + [pl.BlockSpec((ROWS, SLICE), lambda n, h: (0, n)) for _ in parts]
        + [pl.BlockSpec(memory_space=pl.ANY) for _ in into],
        out_specs=pl.BlockSpec((TOK, SLICE), lambda n, h: (0, h * (HALF // SLICE) + first + n)),
        input_output_aliases={3 + len(parts): 0} if into else {},
        compiler_params=pltpu.CompilerParams(vmem_limit_bytes=VMEM),
        cost_estimate=pl.CostEstimate(
            flops=SPAN * 4 * ROWS * TOK * SLICE * tiles, bytes_accessed=2 * (4 * TOK + ROWS) * SLICE * tiles, transcendentals=0
        ),
        name="mix",
    )(*plan, x, *parts, *into)


def shift(x, axis, by):
    n = lax.axis_size(axis)
    return lax.ppermute(x, axis, [(i, (i + by) % n) for i in range(n)])


def labelled(f):
    def call(name, *args):
        with jax.named_scope(name):
            return f(*args)

    return call


@labelled
def exchange(x):
    return lax.all_to_all(x, ("y", "xh"), 0, 0, tiled=True)


@labelled
def gather_ring(x, *first):
    left = shift(x, "z", 1)
    right = shift(x, "z", -1)
    if first:
        left, right, _ = lax.optimization_barrier((left, right, first))
    half = ROWS // 2
    return x, left, right, shift(left[:half], "z", 1), shift(right[half:], "z", -1)


def add(*terms):
    return sum(t.astype(F32) for t in terms).astype(BF16)


def after(x, *others):
    return lax.optimization_barrier((x, others))[0]


@labelled
def scatter_far(far_lo, far_hi):
    return shift(far_lo, "z", 1), shift(far_hi, "z", -1)


def near_kernel(left_ref, right_ref, lo_ref, hi_ref, right_out, left_out):
    half = ROWS // 2
    right_out[:half] = (right_ref[:half].astype(F32) + lo_ref[...].astype(F32)).astype(BF16)
    right_out[half:] = right_ref[half:]
    left_out[:half] = left_ref[:half]
    left_out[half:] = (left_ref[half:].astype(F32) + hi_ref[...].astype(F32)).astype(BF16)


@labelled
def scatter_near(left, right, far):
    spec = lambda n: pl.BlockSpec((n, TILE), lambda i: (0, i))
    right, left = pl.pallas_call(
        near_kernel,
        out_shape=(jax.ShapeDtypeStruct(left.shape, BF16),) * 2,
        grid=(left.shape[1] // TILE,),
        in_specs=[spec(ROWS), spec(ROWS), spec(ROWS // 2), spec(ROWS // 2)],
        out_specs=(spec(ROWS),) * 2,
        compiler_params=pltpu.CompilerParams(vmem_limit_bytes=VMEM),
        cost_estimate=pl.CostEstimate(flops=NEAR * 10**6, bytes_accessed=10 * left.size, transcendentals=0),
        name="near",
    )(left, right, *far)
    return shift(right, "z", 1), shift(left, "z", -1)


def body(
    fwd_boundary,
    grad_boundary,
    saved_inputs,
    routes,
    route_probs,
    capacity,
    roster,
    gate_weight,
    up_weight,
    down_weight,
):
    section = lax.axis_index("pipe")
    sections = lax.axis_size("pipe")
    after_ = (section + 1) % sections
    before = (section + sections - 1) % sections
    take = lambda stack, index: lax.dynamic_index_in_dim(stack, index, 0, keepdims=False)
    fwd_micro = roster[section, 0].reshape(1)
    bwd_micro = roster[section, 1].reshape(1)
    caps = capacity[0]
    route_rows = routes.reshape(2, 1, TOK)
    prob_rows = route_probs.reshape(2, 1, TOK)
    gate_w, up_w, down_w = gate_weight[0, 0], up_weight[0, 0], down_weight[0, 0]

    outgoing = take(fwd_boundary[0], roster[after_, 0])
    layer_input = shift(outgoing, "pipe", 1)
    saved_a, saved_b, bwd_pick = pick(after(bwd_micro, outgoing), caps, route_rows, saved_inputs[0], True)
    own, left, right, far_lo, far_hi = gather_ring("saved_ring_a", saved_a)
    plane_b = exchange("saved_plane_b", saved_b)
    left, right, back_index = lax.optimization_barrier((left, right, roster[before, 1]))
    fwd_rows, _ = pick(fwd_micro, caps, route_rows, after(layer_input, plane_b, left, right)[None], False)
    kept_b = gather_ring("saved_ring_b", plane_b)
    _, left_b, right_b, lo_b, hi_b = kept_b
    fwd_rows, far_lo, far_hi = lax.optimization_barrier((fwd_rows, far_lo, far_hi))
    kept_b = (plane_b, left_b, right_b, lo_b, hi_b)
    grad_input = shift(take(grad_boundary[0], back_index), "pipe", -1)
    input_plane = exchange("input_plane", fwd_rows)
    grad_rows = pick_again(bwd_pick, after(grad_input, fwd_rows, kept_b[1], kept_b[2], far_lo, far_hi))
    grad_plane = exchange("grad_plane", grad_rows)
    wide = jnp.stack([own, left, right, jnp.concatenate([far_lo, far_hi], axis=0)]).reshape(RING, EXPERTS, MSG, TILE)
    wide = wide.transpose(1, 0, 2, 3).reshape(EXPERTS, RING * MSG, TILE)
    kept_a = exchange("saved_plane_a", after(wide, grad_plane))
    gate, up = saved_side((kept_a, *kept_b), gate_w, up_w)
    fwd = gather_ring("input_ring", input_plane, grad_plane)
    own, left, right, far_lo, far_hi = forward_side(fwd, gate_w, up_w, down_w)
    far = scatter_far("output_far", far_lo, far_hi)
    grad = gather_ring("grad_ring", grad_plane, own, gate)
    gate, late_routes = lax.optimization_barrier((gate, route_rows))
    parts = backward_side(grad, gate, up, gate_w, up_w, down_w)
    near = scatter_near("output_near", left, right, far)
    fwd_total = exchange("output_plane", add(own, *near))
    far = scatter_far("back_far", *parts[3:])
    near = scatter_near("back_near", *parts[1:3], far)
    bwd_total = exchange("back_plane", add(parts[0], *near))

    fwd_plan = spread(fwd_micro, caps, late_routes, prob_rows)
    bwd_plan = spread(bwd_micro, caps, late_routes, prob_rows)
    new_output = mix(fwd_plan, (fwd_total,), layer_input)
    new_grad = mix(bwd_plan, (bwd_total,), grad_input)
    return new_output[None], new_grad[None]


def solution(mesh):
    grid = Mesh(mesh.devices.reshape(4, 4, 2, 4), ("pipe", "y", "xh", "z"))
    expert = ("y", "xh", "z")
    rows = P("pipe", None, expert, None)
    weight = P("pipe", expert, None, None)
    in_specs = (rows,) * 5 + (P("pipe", None), P()) + (weight,) * 3
    out_specs = (P("pipe", expert, None),) * 2
    return jax.shard_map(body, mesh=grid, in_specs=in_specs, out_specs=out_specs, check_vma=False)
```
